128 devices in a mesh: gx: 8 (over x, z_hi), gy: 16 (over z_lo, y, core).
Axes of the slice: x: 4, y: 4, z: 4 (z_hi: 2, z_lo: 2; z = z_hi * 2 + z_lo), core: 2. Of those that a mesh axis runs over, the one named last changes fastest.
Arguments:
- flow_state: float32 [4, 2048, 4096], P(None, 'gx', 'gy'), may hold values from -0.4 to 3.5, as said below
- cell_kind: int32 [2048, 4096], P('gx', 'gy'), may hold values from 0 to 2
Outputs:
- new_state: float32 [4, 2048, 4096], P(None, 'gx', 'gy')
- fine_residual: float32 [4, 2048, 4096], P(None, 'gx', 'gy')
The draws below stay inside these ranges and needn't reach their ends.
Inputs may be any that keep to these rules, and one draw needn't show every extreme that they name: `flow_state`: every cell holds the conserved variables of a state with density 0.8 to 1.25, velocity components -0.3 to 0.3 and pressure 0.7 to 1.3.
All inputs are finite; a program needn't handle non-finite values.
Results may differ from the reference program's by a relative error of at most 0.00002.
Values sent between devices are 32-bit elements; how exact they have to be, the bound alone decides.
A program may use at most 64 MiB of HBM per device.

```python
import jax
import jax.numpy as jnp
from jax import lax

NX = 2048
NY = 4096


def draw_flow_state(key, part):
    keys = jax.random.split(key, 4)
    rough_density = jax.random.uniform(keys[0], (NX, NY), jnp.float32, -1.0, 1.0)
    rough_x = jax.random.uniform(keys[1], (NX, NY), jnp.float32, -1.0, 1.0)
    rough_y = jax.random.uniform(keys[2], (NX, NY), jnp.float32, -1.0, 1.0)
    rough_press = jax.random.uniform(keys[3], (NX, NY), jnp.float32, -1.0, 1.0)
    density = 1.025 + 0.225 * rough_density
    speed_x = 0.3 * rough_x
    speed_y = 0.3 * rough_y
    pressure = 1.0 + 0.3 * rough_press
    energy = pressure / 0.4 + 0.5 * density * (speed_x * speed_x + speed_y * speed_y)
    return jnp.stack([density, density * speed_x, density * speed_y, energy], 0).astype(jnp.float32)


def with_ends(values, own_key, smallest, top_value):
    extent = values.shape
    spot = [jax.random.randint(jax.random.fold_in(own_key, axis), (), 0, extent[axis]) for axis in range(len(extent))]
    values = values.at[tuple(spot)].set(smallest)
    longest = extent.index(max(extent))
    spot[longest] = (spot[longest] + 1) % extent[longest]
    return values.at[tuple(spot)].set(top_value)


def setup_inputs(seed: int = 0) -> dict:
    splits = jax.random.split(jax.random.key(seed), 3)
    return {
        "flow_state": draw_flow_state(jax.random.fold_in(splits[2], 71), 0),
        "cell_kind": with_ends(jax.random.randint(splits[1], (NX, NY), 0, 3), jax.random.fold_in(splits[1], 1), 0, 2).astype(jnp.int32),
    }


courant = 0.4
kappa_two = 0.25
kappa_four = 1.0 / 32.0

def section(field, start, stop, axis_dim):
    return lax.slice_in_dim(field, start, stop, axis=axis_dim)

def sweep(strip_cells, normal, axis_dim):
    length = strip_cells.shape[axis_dim] - 4
    density = strip_cells[0:1]
    momentum_x = strip_cells[1:2]
    momentum_y = strip_cells[2:3]
    energy = strip_cells[3:4]
    inverse = 1.0 / density
    speed_x = momentum_x * inverse
    speed_y = momentum_y * inverse
    pressure = 0.4 * (energy - 0.5 * (momentum_x * speed_x + momentum_y * speed_y))
    if normal == 1:
        normal_speed = speed_x
        flux = jnp.concatenate([momentum_x, momentum_x * speed_x + pressure, momentum_y * speed_x, (energy + pressure) * speed_x], 0)
    else:
        normal_speed = speed_y
        flux = jnp.concatenate([momentum_y, momentum_x * speed_y, momentum_y * speed_y + pressure, (energy + pressure) * speed_y], 0)
    spectral = jnp.abs(normal_speed) + jnp.sqrt(1.4 * pressure * inverse)
    press_low = section(pressure, 0, length + 2, axis_dim)
    press_mid = section(pressure, 1, length + 3, axis_dim)
    press_high = section(pressure, 2, length + 4, axis_dim)
    sensor = jnp.abs(press_high - 2.0 * press_mid + press_low) / (press_high + 2.0 * press_mid + press_low)
    second_coef = kappa_two * jnp.maximum(section(sensor, 0, length + 1, axis_dim), section(sensor, 1, length + 2, axis_dim))
    fourth_coef = jnp.maximum(0.0, kappa_four - second_coef)
    cell_back = section(strip_cells, 0, length + 1, axis_dim)
    cell_left = section(strip_cells, 1, length + 2, axis_dim)
    cell_right = section(strip_cells, 2, length + 3, axis_dim)
    cell_ahead = section(strip_cells, 3, length + 4, axis_dim)
    face_spectral = 0.5 * (section(spectral, 1, length + 2, axis_dim) + section(spectral, 2, length + 3, axis_dim))
    central = 0.5 * (section(flux, 1, length + 2, axis_dim) + section(flux, 2, length + 3, axis_dim))
    damping = second_coef * (cell_right - cell_left) - fourth_coef * (cell_ahead - 3.0 * cell_right + 3.0 * cell_left - cell_back)
    face_flux = central - face_spectral * damping
    divergence = section(face_flux, 1, length + 1, axis_dim) - section(face_flux, 0, length, axis_dim)
    return (divergence, section(spectral, 2, length + 2, axis_dim))

def residual(strip_x, strip_y, wall_share, far_share, spacing):
    div_x, spec_x = sweep(strip_x, 1, 1)
    div_y, spec_y = sweep(strip_y, 2, 2)
    cells = strip_x[:, 2:-2, :]
    free_stream = jnp.array([1.0, 0.5, 0.0, 1.0 / 0.56 + 0.125], dtype=jnp.float32).reshape(4, 1, 1)
    momentum_rate = jnp.array([0.0, 2.0, 2.0, 0.0], dtype=jnp.float32).reshape(4, 1, 1)
    source = wall_share[None] * momentum_rate * cells + far_share[None] * (cells - free_stream)
    return (spacing * (div_x + div_y) + spacing * spacing * source, spec_x + spec_y)

def periodic(field):
    padded = jnp.pad(field, ((0, 0), (2, 2), (2, 2)), mode='wrap')
    return (padded[:, :, 2:-2], padded[:, 2:-2, :])

def coarse(field):
    comps, rows, cols = field.shape
    return field.reshape(comps, rows // 2, 2, cols // 2, 2).sum(axis=(2, 4))

def reference(flow_state, cell_kind):
    wall_share = (cell_kind == 1).astype(jnp.float32)
    far_share = (cell_kind == 2).astype(jnp.float32)
    strip_x, strip_y = periodic(flow_state)
    start_residual, start_spectral = residual(strip_x, strip_y, wall_share, far_share, 1.0)
    smoothed = flow_state - courant / start_spectral * start_residual
    strip_x, strip_y = periodic(smoothed)
    fine_residual, unused_spec = residual(strip_x, strip_y, wall_share, far_share, 1.0)
    coarse_state = 0.25 * coarse(smoothed)
    coarse_sum = coarse(fine_residual)
    coarse_wall = 0.25 * coarse(wall_share[None])[0]
    coarse_far = 0.25 * coarse(far_share[None])[0]
    strip_x, strip_y = periodic(coarse_state)
    coarse_start, coarse_spectral = residual(strip_x, strip_y, coarse_wall, coarse_far, 2.0)
    forcing = coarse_sum - coarse_start
    coarse_segment = coarse_state - courant / coarse_spectral * coarse_sum * 0.5
    strip_x, strip_y = periodic(coarse_segment)
    segment_residual, unused_more = residual(strip_x, strip_y, coarse_wall, coarse_far, 2.0)
    coarse_final = coarse_state - courant / coarse_spectral * (segment_residual + forcing) * 0.5
    correction = coarse_final - coarse_state
    fine_add = jnp.repeat(jnp.repeat(correction, 2, axis=1), 2, axis=2)
    return (smoothed + fine_add, fine_residual)
```

```python
import jax
import jax.numpy as jnp
from jax import lax
from jax.experimental import pallas as pl
from jax.experimental.pallas import tpu as pltpu
from jax.sharding import PartitionSpec as P

MESH = pl.DeviceIdType.MESH
LANES = 128
SUB = 8
HALO = 8
STRIP = 24

WINF_R = (1.0, 0.5, 0.0, 1.0 / 0.56 + 0.125)
WINF_C = (1.0, 0.0, 0.5, 1.0 / 0.56 + 0.125)


def lane_index():
    return lax.broadcasted_iota(jnp.int32, (SUB, LANES), 1)


def lane_roll(v, shift):
    return pltpu.roll(v, shift % LANES, 1)


def sub_roll(v, shift):
    return pltpu.roll(v, shift % SUB, 0)


def shift_pair(vals, k):
    lane = lane_index()
    a, b = (lane_roll(v, -k) for v in vals)
    inside = lane < LANES - 1 if k == 1 else lane > 0
    return [jnp.where(inside, a, b), jnp.where(inside, b, a)]


def shift_packed(vals, k):
    lane = lane_index()
    (v,) = vals
    if k == 1:
        return [jnp.where(lane >= LANES - 2, lane_roll(v, -3), lane_roll(v, -2))]
    return [jnp.where(lane < 2, lane_roll(v, 3), lane_roll(v, 2))]


def make_strip_shift(step):
    def shift(vals, k):
        lane = lane_index()
        (v,) = vals
        a = lane_roll(v, -k * step)
        b = sub_roll(a, -2 * k)
        outside = lane >= LANES - step if k == 1 else lane < step
        return [jnp.where(outside, b, a)]

    return shift


shift_strip = make_strip_shift(1)
shift_strip_coarse = make_strip_shift(2)


def loop(lo, hi, unroll, body):
    count = hi - lo
    while count % unroll:
        unroll -= 1

    def run(step, carry):
        for i in range(unroll):
            carry = body(lo + step * unroll + i, carry)
        return carry

    return lambda carry: lax.fori_loop(0, count // unroll, run, carry)


def primitives(w_ref, p_ref, tiles, lo, hi, unroll=4):
    def body(r, carry):
        for t in range(tiles):
            density, mom_r, mom_l, energy = (w_ref[t, c, r] for c in range(4))
            inverse = 1.0 / density
            u = mom_r * inverse
            v = mom_l * inverse
            press = 0.4 * (energy - 0.5 * (mom_r * u + mom_l * v))
            p_ref[t, 0, r] = press
            p_ref[t, 1, r] = u
            p_ref[t, 2, r] = v
            p_ref[t, 3, r] = jnp.sqrt(1.4 * press * inverse)
        return carry

    loop(lo, hi, unroll, body)(0)


def face_coefs(sensor_a, sensor_b, spec_a, spec_b):
    second = jnp.maximum(sensor_a, sensor_b)
    fourth = jnp.maximum(0.0, 1.0 / 32.0 - second)
    total = spec_a + spec_b
    coef_b = total * fourth
    coef_a = total * second + 2.0 * coef_b
    return coef_a, coef_b


def quarter_sensor(low, mid, high):
    ends = low + high
    twice = 2.0 * mid
    return 0.25 * jnp.abs(ends - twice) / (ends + twice)


def along_rows(w_ref, p_ref, d_ref, tiles, lo, hi, unroll=8):
    def flux(t, r):
        w = [w_ref[t, c, r] for c in range(4)]
        press, q, sound = p_ref[t, 0, r], p_ref[t, 1, r], p_ref[t, 3, r]
        f = [w[1], w[1] * q + press, w[2] * q, (w[3] + press) * q]
        return f, jnp.abs(q) + sound

    def sensor(t, r):
        return quarter_sensor(p_ref[t, 0, r - 1], p_ref[t, 0, r], p_ref[t, 0, r + 1])

    def diff(t, r):
        return [w_ref[t, c, r + 1] - w_ref[t, c, r] for c in range(4)]

    def face(t, r, d_back, d_here, f_here, s_here, n_here):
        d_next = diff(t, r + 1)
        f_next, s_next = flux(t, r + 1)
        n_next = sensor(t, r + 1)
        ca, cb = face_coefs(n_here, n_next, s_here, s_next)
        h = [
            f_here[c] + f_next[c] - ca * d_here[c] + cb * (d_next[c] + d_back[c])
            for c in range(4)
        ]
        return h, d_next, f_next, s_next, n_next

    for t in range(tiles):
        d_back = diff(t, lo - 2)
        d_here = diff(t, lo - 1)
        f_here, s_here = flux(t, lo - 1)
        n_here = sensor(t, lo - 1)
        h, d_next, f_next, s_next, n_next = face(t, lo - 1, d_back, d_here, f_here, s_here, n_here)

        def body(r, carry):
            h_back, d_back, d_here, f_here, s_here, n_here = carry
            h, d_next, f_next, s_next, n_next = face(t, r, d_back, d_here, f_here, s_here, n_here)
            for c in range(4):
                d_ref[t, c, r] = h[c] - h_back[c]
            return h, d_here, d_next, f_next, s_next, n_next

        loop(lo, hi, unroll, body)((h, d_here, d_next, f_next, s_next, n_next))


def along_lanes(w_ref, p_ref, d_ref, tiles, lo, hi, shift, emit, unroll=2):
    every = range(tiles)

    def body(r, carry):
        w = [[w_ref[t, c, r] for t in every] for c in range(4)]
        press = [p_ref[t, 0, r] for t in every]
        q = [p_ref[t, 2, r] for t in every]
        spec = [jnp.abs(q[t]) + p_ref[t, 3, r] for t in every]
        w_up = [shift(w[c], 1) for c in range(4)]
        p_up, p_down = shift(press, 1), shift(press, -1)
        q_up = shift(q, 1)
        s_up = shift(spec, 1)
        sens = [quarter_sensor(p_down[t], press[t], p_up[t]) for t in every]
        n_up = shift(sens, 1)
        coefs = [face_coefs(sens[t], n_up[t], spec[t], s_up[t]) for t in every]
        out = []
        for c in range(4):
            d = [w_up[c][t] - w[c][t] for t in every]
            d_up, d_down = shift(d, 1), shift(d, -1)
            h = []
            for t in every:
                if c == 0:
                    f = w[2][t] + w_up[2][t]
                elif c == 1:
                    f = w[1][t] * q[t] + w_up[1][t] * q_up[t]
                elif c == 2:
                    f = (w[2][t] * q[t] + press[t]) + (w_up[2][t] * q_up[t] + p_up[t])
                else:
                    f = (w[3][t] + press[t]) * q[t] + (w_up[3][t] + p_up[t]) * q_up[t]
                h.append(f - coefs[t][0] * d[t] + coefs[t][1] * (d_up[t] + d_down[t]))
            h_down = shift(h, -1)
            out.append([(h[t] - h_down[t]) + d_ref[t, c, r] for t in every])
        emit(r, w, out)
        return carry

    loop(lo, hi, unroll, body)(0)


def with_source(w, total, wall, far, winf, half_h, h_square):
    if h_square != 1.0:
        wall, far = h_square * wall, h_square * far
    both = 2.0 * wall + far
    out = []
    for c in range(4):
        base = total[c] if half_h == 1.0 else half_h * total[c]
        weight = both if c in (1, 2) else far
        term = weight * w[c]
        if winf[c] != 0.0:
            term = term - far * winf[c]
        out.append(base + term)
    return out


def spectral_sum(p_ref, t, r):
    return jnp.abs(p_ref[t, 1, r]) + jnp.abs(p_ref[t, 2, r]) + 2.0 * p_ref[t, 3, r]


def leg(refs, tiles, shift, shift_coarse, restrict_lanes, winf, rows, refresh, coarse_tiles=1):
    w, pr, dx, sm, fr, kind, cs, cpr, cdx, csum, kk, seg, forc, corr, share = refs
    (p1, s1, p2, s2, c_state, c_seg, c_out) = rows

    def smooth(r, w_vals, total):
        for t in range(tiles):
            wall = jnp.where(kind[t, r] == 1.0, 1.0, 0.0)
            far = jnp.where(kind[t, r] == 2.0, 1.0, 0.0)
            mine = [w_vals[c][t] for c in range(4)]
            res = with_source(mine, [total[c][t] for c in range(4)], wall, far, winf, 0.5, 1.0)
            scale = 0.4 / spectral_sum(pr, t, r)
            for c in range(4):
                sm[t, c, r] = mine[c] - scale * res[c]

    def fine(r, w_vals, total):
        for t in range(tiles):
            wall = jnp.where(kind[t, r] == 1.0, 1.0, 0.0)
            far = jnp.where(kind[t, r] == 2.0, 1.0, 0.0)
            mine = [w_vals[c][t] for c in range(4)]
            res = with_source(mine, [total[c][t] for c in range(4)], wall, far, winf, 0.5, 1.0)
            for c in range(4):
                fr[t, c, r] = res[c]

    primitives(w, pr, tiles, *p1)
    along_rows(w, pr, dx, tiles, *s1)
    yield "rows"
    along_lanes(w, pr, dx, tiles, *s1, shift, smooth)
    refresh(sm, tiles)
    yield "smoothed"
    primitives(sm, pr, tiles, *p2)
    along_rows(sm, pr, dx, tiles, *s2)
    along_lanes(sm, pr, dx, tiles, *s2, shift, fine)
    yield "fine"

    def state(k, carry):
        for c in range(4):
            cs[0, c, k] = 0.25 * restrict_lanes([sm[t, c, 2 * k + off] + sm[t, c, 2 * k + off + 1] for t in range(tiles)])
        return carry

    off = -2 if tiles == 2 else 0
    loop(*c_state, 2, state)(0)
    refresh(cs, 1)

    def sums(k, carry):
        for c in range(4):
            csum[0, c, k] = restrict_lanes([fr[t, c, 2 * k + off] + fr[t, c, 2 * k + off + 1] for t in range(tiles)])
        for i, code in enumerate((1.0, 2.0)):
            share[0, i, k] = 0.25 * restrict_lanes(
                [
                    jnp.where(kind[t, 2 * k + off] == code, 1.0, 0.0)
                    + jnp.where(kind[t, 2 * k + off + 1] == code, 1.0, 0.0)
                    for t in range(tiles)
                ]
            )
        return carry

    loop(*c_seg, 2, sums)(0)
    wide = (0, 20) if tiles == 2 else c_seg
    primitives(cs, cpr, 1, *wide)

    def segment(k, carry):
        scale = 0.2 / spectral_sum(cpr, 0, k)
        kk[0, k] = scale
        for c in range(4):
            seg[0, c, k] = cs[0, c, k] - scale * csum[0, c, k]
        return carry

    loop(*c_seg, 4, segment)(0)
    refresh(seg, 1)

    def force(k, w_vals, total):
        res = with_source([v[0] for v in w_vals], [v[0] for v in total], share[0, 0, k], share[0, 1, k], winf, 1.0, 4.0)
        for c in range(4):
            forc[0, c, k] = csum[0, c, k] - res[c]

    along_rows(cs, cpr, cdx, 1, *c_out)
    along_lanes(cs, cpr, cdx, 1, *c_out, shift_coarse, force)
    primitives(seg, cpr, 1, *wide)

    def final(k, w_vals, total):
        res = with_source([v[0] for v in w_vals], [v[0] for v in total], share[0, 0, k], share[0, 1, k], winf, 1.0, 4.0)
        for c in range(4):
            corr[0, c, k] = -kk[0, k] * (res[c] + forc[0, c, k])

    along_rows(seg, cpr, cdx, 1, *c_out)
    along_lanes(seg, cpr, cdx, 1, *c_out, shift_coarse, final)
    yield "done"


MAIN_ROWS = ((0, 36), (2, 34), (0, 36), (2, 34), (2, 18), (2, 18), (2, 18))
STRIP_ROWS = ((0, 24), (2, 22), (2, 22), (4, 20), (1, 11), (2, 10), (4, 8))


def restrict_pair(vals):
    lane = lane_index()
    a, b = vals
    return jnp.where(lane % 2 == 0, a + lane_roll(a, -1), b + lane_roll(b, 1))


def restrict_strip(vals):
    lane = lane_index()
    (a,) = vals
    return a + jnp.where(lane % 2 == 0, lane_roll(a, -1), lane_roll(a, 1))


def refresh_main(ref, tiles):
    depth = ref.shape[2]
    for t in range(tiles):
        for c in range(4):
            for i in range(2):
                ref[t, c, i] = sub_roll(ref[t, c, depth - 4 + i], 1)
                ref[t, c, depth - 2 + i] = sub_roll(ref[t, c, 2 + i], -1)


def no_refresh(ref, tiles):
    pass


def run_to(steps, name):
    for reached in steps:
        if reached == name:
            return


T_L, B_L, T_0, B_0, T_1, B_1, T_R, B_R = range(8)
L_0, R_0, L_1, R_1 = range(4)


def kernel(nx, ny, flow_hbm, kind_hbm, new_hbm, res_hbm, inb, kb, rowbuf, rowkind, colbuf, pack, got, out_new, out_res,
           row_out, col_out, *rest):
    main_refs, strip_refs, (load_sem, send_sem, recv_sem, store_sem) = rest[:15], rest[15:30], rest[30:]
    gx, gy = lax.axis_index("gx"), lax.axis_index("gy")
    up, down = lax.rem(gx + nx - 1, nx), lax.rem(gx + 1, nx)
    left, right = lax.rem(gy + ny - 1, ny), lax.rem(gy + 1, ny)
    neighbours = [(up, gy), (down, gy), (gx, left), (gx, right), (up, left), (up, right), (down, left), (down, right)]

    loads = []
    for t in range(2):
        cols = pl.ds(t * LANES, LANES)
        loads.append(pltpu.make_async_copy(flow_hbm.at[:, :, cols], inb.at[t], load_sem.at[2 * t]))
        loads.append(pltpu.make_async_copy(kind_hbm.at[:, cols], kb.at[t], load_sem.at[2 * t + 1]))
    for copy in loads:
        copy.start()

    barrier = pltpu.get_barrier_semaphore()
    for where in neighbours:
        pl.semaphore_signal(barrier, inc=1, device_id=where, device_id_type=MESH)
    for copy in loads:
        copy.wait()

    lane = lane_index()

    for side in range(2):
        for i, row in enumerate((0, 8, 240, 248)):
            rows = pl.ds(row, 8)
            total = None
            for c in range(5):
                v = kb[side, rows, :].astype(jnp.float32) if c == 4 else inb[side, c, rows, :]
                if side:
                    v = lane_roll(v, -8 * c)
                    total = v if c == 0 else jnp.where(lane < LANES - 8 * c, v, total)
                else:
                    v = lane_roll(v, 8 * c)
                    total = v if c == 0 else jnp.where(lane >= 8 * c, v, total)
            pack[side, pl.ds(8 * i, 8), :] = total

    for c, source in enumerate((0, 2, 1, 3, 4)):
        for side in range(2):
            for half in range(2):
                rows = pl.ds(half * LANES, LANES)
                v = kb[side, rows, :].astype(jnp.float32) if c == 4 else inb[side, source, rows, :]
                turned = v.T
                seg = half * 2 + side
                if side:
                    colbuf[c, pl.ds(seg * STRIP, 16), :] = turned[112:128]
                else:
                    colbuf[c, pl.ds(seg * STRIP + 8, 16), :] = turned[0:16]

    for t, (top, bottom) in enumerate(((T_0, B_0), (T_1, B_1))):
        for c in range(4):
            rowbuf[c, pl.ds(top * STRIP + 8, 16), :] = inb[t, c, pl.ds(0, 16), :]
            rowbuf[c, pl.ds(bottom * STRIP, 16), :] = inb[t, c, pl.ds(240, 16), :]
        rowbuf[4, pl.ds(top * STRIP + 8, 16), :] = kb[t, pl.ds(0, 16), :].astype(jnp.float32)
        rowbuf[4, pl.ds(bottom * STRIP, 16), :] = kb[t, pl.ds(240, 16), :].astype(jnp.float32)

    w_main, kind_main = main_refs[0], main_refs[5]

    def relayout(r, carry):
        for t in range(2):
            for c in range(4):
                w_main[t, c, r + 2] = inb[t, c, pl.ds(r, SUB, stride=32), :]
            kind_main[t, r + 2] = kb[t, pl.ds(r, SUB, stride=32), :].astype(jnp.float32)
        return carry

    loop(0, 32, 4, relayout)(0)
    refresh_main(w_main, 2)

    main = leg(main_refs, 2, shift_pair, shift_packed, restrict_pair, WINF_R, MAIN_ROWS, refresh_main)
    run_to(main, "rows")

    pl.semaphore_wait(barrier, 8)
    number = 0
    copies = []

    def send(src, dst, where):
        nonlocal number
        copy = pltpu.make_async_remote_copy(
            src_ref=src, dst_ref=dst, send_sem=send_sem.at[number], recv_sem=recv_sem.at[number],
            device_id=where, device_id_type=MESH)
        copy.start()
        copies.append(copy)
        number += 1

    low, high = pl.ds(0, 8), pl.ds(248, 8)
    send(pack.at[1, pl.ds(24, 8)], got.at[0, pl.ds(0, 8)], (down, right))
    send(pack.at[0, pl.ds(24, 8)], got.at[1, pl.ds(0, 8)], (down, left))
    send(pack.at[1, pl.ds(0, 8)], got.at[0, pl.ds(40, 8)], (up, right))
    send(pack.at[0, pl.ds(0, 8)], got.at[1, pl.ds(40, 8)], (up, left))
    for t, (top, bottom) in enumerate(((T_0, B_0), (T_1, B_1))):
        send(inb.at[t, :, high, :], rowbuf.at[pl.ds(0, 4), pl.ds(top * STRIP, 8), :], (down, gy))
        send(inb.at[t, :, low, :], rowbuf.at[pl.ds(0, 4), pl.ds(bottom * STRIP + 16, 8), :], (up, gy))
    send(kb.at[:, high, :], rowkind.at[0], (down, gy))
    send(kb.at[:, low, :], rowkind.at[1], (up, gy))
    send(pack.at[1], got.at[0, pl.ds(8, 32)], (gx, right))
    send(pack.at[0], got.at[1, pl.ds(8, 32)], (gx, left))
    first_column = number
    for to_left, to_right in ((L_0, R_0), (L_1, R_1)):
        send(colbuf.at[:, pl.ds(to_right * STRIP + 8, 8), :], colbuf.at[:, pl.ds(to_left * STRIP, 8), :], (gx, right))
        send(colbuf.at[:, pl.ds(to_left * STRIP + 8, 8), :], colbuf.at[:, pl.ds(to_right * STRIP + 16, 8), :], (gx, left))

    run_to(main, "done")
    sm_main, fr_main, corr_main = main_refs[3], main_refs[4], main_refs[13]

    def finish(k, carry):
        for c in range(4):
            v = corr_main[0, c, k + 2]
            even = lane_index() % 2 == 0
            add = [jnp.where(even, v, lane_roll(v, 1)), jnp.where(even, lane_roll(v, -1), v)]
            for t in range(2):
                for i in range(2):
                    r = 2 * k + i
                    out_new[t, c, pl.ds(r, SUB, stride=32), :] = sm_main[t, c, r + 2] + add[t]
                    out_res[t, c, pl.ds(r, SUB, stride=32), :] = fr_main[t, c, r + 2]
        return carry

    loop(0, 16, 2, finish)(0)

    w_strip, sm_strip, fr_strip, kind_strip, corr_strip = (strip_refs[i] for i in (0, 3, 4, 5, 13))

    def gather(buf):
        def body(r, carry):
            for c in range(4):
                w_strip[0, c, r] = buf[c, pl.ds(r, SUB, stride=STRIP), :]
            kind_strip[0, r] = buf[4, pl.ds(r, SUB, stride=STRIP), :]
            return carry

        loop(0, STRIP, 4, body)(0)

    for copy in copies[first_column:]:
        copy.wait_recv()
    gather(colbuf)
    run_to(leg(strip_refs, 1, shift_strip, shift_strip_coarse, restrict_strip, WINF_C, STRIP_ROWS, no_refresh), "done")

    def column_out(i, carry):
        for c, target in enumerate((0, 2, 1, 3)):
            col_out[pl.ds(target * 8 + i, SUB, stride=64), :] = sm_strip[0, c, i + 8] + corr_strip[0, c, (i + 8) // 2]
            col_out[pl.ds((target + 4) * 8 + i, SUB, stride=64), :] = fr_strip[0, c, i + 8]
        return carry

    loop(0, 8, 2, column_out)(0)
    for half in range(2):
        turned = col_out[pl.ds(half * LANES, LANES), :].T

        for a in range(8):
            ref, c = (out_new, a) if a < 4 else (out_res, a - 4)
            rows = pl.ds(half * LANES, LANES)
            wide = lax.broadcasted_iota(jnp.int32, (LANES, LANES), 1)
            ref[0, c, rows, :] = jnp.where(wide < 8, pltpu.roll(turned, (-8 * a) % LANES, 1), ref[0, c, rows, :])
            ref[1, c, rows, :] = jnp.where(wide >= 120, pltpu.roll(turned, (56 - 8 * a) % LANES, 1), ref[1, c, rows, :])

    stores = []

    def store(src, dst):
        copy = pltpu.make_async_copy(src, dst, store_sem.at[len(stores)])
        copy.start()
        stores.append(copy)

    inner = pl.ds(8, 240)
    for t in range(2):
        cols = pl.ds(t * LANES, LANES)
        store(out_new.at[t, :, inner, :], new_hbm.at[:, inner, cols])
        store(out_res.at[t, :, inner, :], res_hbm.at[:, inner, cols])

    for copy in copies[:first_column]:
        copy.wait_recv()
    for side, (top, bottom) in enumerate(((T_L, B_L), (T_R, B_R))):
        for j, seg in enumerate((top, bottom)):
            for i in range(3):
                v = got[side, pl.ds(24 * j + 8 * i, 8), :]
                for c in range(5):
                    rowbuf[c, pl.ds(seg * STRIP + 8 * i, 8), :] = lane_roll(v, -8 * c if side else 8 * c)
    for t, (top, bottom) in enumerate(((T_0, B_0), (T_1, B_1))):
        rowbuf[4, pl.ds(top * STRIP, 8), :] = rowkind[0, t].astype(jnp.float32)
        rowbuf[4, pl.ds(bottom * STRIP + 16, 8), :] = rowkind[1, t].astype(jnp.float32)
    gather(rowbuf)
    run_to(leg(strip_refs, 1, shift_strip, shift_strip_coarse, restrict_strip, WINF_R, STRIP_ROWS, no_refresh), "done")

    def row_result(i, carry):
        for c in range(4):
            row_out[0, c, pl.ds(i, SUB, stride=8), :] = sm_strip[0, c, i + 8] + corr_strip[0, c, (i + 8) // 2]
            row_out[1, c, pl.ds(i, SUB, stride=8), :] = fr_strip[0, c, i + 8]
        return carry

    loop(0, 8, 2, row_result)(0)
    for a, out in enumerate((new_hbm, res_hbm)):
        for t, (top, bottom) in enumerate(((T_0, B_0), (T_1, B_1))):
            cols = pl.ds(t * LANES, LANES)
            store(row_out.at[a, :, pl.ds(top * 8, 8), :], out.at[:, low, cols])
            store(row_out.at[a, :, pl.ds(bottom * 8, 8), :], out.at[:, high, cols])
    for copy in copies:
        copy.wait_send()
    for copy in stores:
        copy.wait()


def vmem(*shape):
    return pltpu.VMEM(shape, jnp.float32)


def domain(tiles, rows, coarse_rows):
    tile = (SUB, LANES)
    return [
        vmem(tiles, 4, rows, *tile),
        vmem(tiles, 4, rows, *tile),
        vmem(tiles, 4, rows, *tile),
        vmem(tiles, 4, rows, *tile),
        vmem(tiles, 4, rows, *tile),
        vmem(tiles, rows, *tile),
        vmem(1, 4, coarse_rows, *tile),
        vmem(1, 4, coarse_rows, *tile),
        vmem(1, 4, coarse_rows, *tile),
        vmem(1, 4, coarse_rows, *tile),
        vmem(1, coarse_rows, *tile),
        vmem(1, 4, coarse_rows, *tile),
        vmem(1, 4, coarse_rows, *tile),
        vmem(1, 4, coarse_rows, *tile),
        vmem(1, 2, coarse_rows, *tile),
    ]


def solution(mesh):
    nx, ny = mesh.shape["gx"], mesh.shape["gy"]

    def local(flow_state, cell_kind):
        import functools

        out = jax.ShapeDtypeStruct(flow_state.shape, jnp.float32)
        hbm = pl.BlockSpec(memory_space=pl.ANY)
        return pl.pallas_call(
            functools.partial(kernel, nx, ny),
            out_shape=(out, out),
            in_specs=[hbm, hbm],
            out_specs=(hbm, hbm),
            scratch_shapes=[
                vmem(2, 4, 256, LANES),
                pltpu.VMEM((2, 256, LANES), jnp.int32),
                vmem(5, 8 * STRIP, LANES),
                pltpu.VMEM((2, 2, 8, LANES), jnp.int32),
                vmem(5, 8 * STRIP, LANES),
                vmem(2, 32, LANES),
                vmem(2, 48, LANES),
                vmem(2, 4, 256, LANES),
                vmem(2, 4, 256, LANES),
                vmem(2, 4, 64, LANES),
                vmem(512, LANES),
                *domain(2, 36, 20),
                *domain(1, 24, 12),
                pltpu.SemaphoreType.DMA((4,)),
                pltpu.SemaphoreType.DMA((16,)),
                pltpu.SemaphoreType.DMA((16,)),
                pltpu.SemaphoreType.DMA((12,)),
            ],
            compiler_params=pltpu.CompilerParams(collective_id=0, has_side_effects=True),
        )(flow_state, cell_kind)

    return jax.shard_map(
        local,
        mesh=mesh,
        in_specs=(P(None, "gx", "gy"), P("gx", "gy")),
        out_specs=(P(None, "gx", "gy"), P(None, "gx", "gy")),
        check_vma=False,
    )
```

```python
import functools

import jax
import jax.numpy as jnp
from jax import lax
from jax.experimental import pallas as pl
from jax.experimental.pallas import tpu as pltpu
from jax.sharding import PartitionSpec as P

MESH = pl.DeviceIdType.MESH
LANES = 128
SUB = 8
ROWS = 32
STRIP = 24

ENERGY = 1.0 / 0.56 + 0.125

LEFT, RIGHT, TOP_L, TOP, TOP_R, BOT_L, BOT, BOT_R = range(8)

FINE_UNROLL = 2
ROW_UNROLL = 8
COARSE_UNROLL = 4


def lane_index():
    return lax.broadcasted_iota(jnp.int32, (SUB, LANES), 1)


def sub_index():
    return lax.broadcasted_iota(jnp.int32, (SUB, LANES), 0)


def sub_roll(v, shift):
    return pltpu.roll(v, shift % SUB, 0)


def take(v, index):
    return jnp.take_along_axis(v, index, axis=1)


def ahead_main(v, k):
    return pltpu.roll(v, -k % LANES, 1)


def ahead_strip(v, k):
    here = pltpu.roll(v, -k % LANES, 1)
    lane = lane_index()
    if k > 0:
        return jnp.where(lane >= LANES - k, sub_roll(here, -1), here)
    return jnp.where(lane < -k, sub_roll(here, 1), here)


def loop(lo, hi, unroll, body, carry=0):
    count = hi - lo
    while count % unroll:
        unroll -= 1

    def run(step, carry):
        for i in range(unroll):
            carry = body(lo + step * unroll + i, carry)
        return carry

    return lax.fori_loop(0, count // unroll, run, carry)


def primitives(w_ref, p_ref, tiles, lo, hi, unroll=4):
    def body(r, carry):
        for t in range(tiles):
            density, mom_r, mom_l, energy = (w_ref[t, c, r] for c in range(4))
            inverse = 1.0 / density
            u = mom_r * inverse
            v = mom_l * inverse
            press = 0.4 * (energy - 0.5 * (mom_r * u + mom_l * v))
            p_ref[t, 0, r] = press
            p_ref[t, 1, r] = u
            p_ref[t, 2, r] = v
            p_ref[t, 3, r] = jnp.sqrt(1.4 * press * inverse)
        return carry

    loop(lo, hi, unroll, body)


def face_coefs(sensor_a, sensor_b, spec_a, spec_b):
    second = jnp.maximum(sensor_a, sensor_b)
    fourth = jnp.maximum(0.0, 1.0 / 32.0 - second)
    total = spec_a + spec_b
    coef_b = total * fourth
    coef_a = total * second + 2.0 * coef_b
    return coef_a, coef_b


def quarter_sensor(low, mid, high):
    ends = low + high
    twice = 2.0 * mid
    return 0.25 * jnp.abs(ends - twice) / (ends + twice)


def along_rows(w_ref, p_ref, d_ref, tiles, lo, hi, unroll):
    def flux(t, r):
        w = [w_ref[t, c, r] for c in range(4)]
        press, q, sound = p_ref[t, 0, r], p_ref[t, 1, r], p_ref[t, 3, r]
        f = [w[1], w[1] * q + press, w[2] * q, (w[3] + press) * q]
        return f, jnp.abs(q) + sound

    def sensor(t, r):
        return quarter_sensor(p_ref[t, 0, r - 1], p_ref[t, 0, r], p_ref[t, 0, r + 1])

    def diff(t, r):
        return [w_ref[t, c, r + 1] - w_ref[t, c, r] for c in range(4)]

    def face(t, r, d_back, d_here, f_here, s_here, n_here):
        d_next = diff(t, r + 1)
        f_next, s_next = flux(t, r + 1)
        n_next = sensor(t, r + 1)
        ca, cb = face_coefs(n_here, n_next, s_here, s_next)
        h = [
            f_here[c] + f_next[c] - ca * d_here[c] + cb * (d_next[c] + d_back[c])
            for c in range(4)
        ]
        return h, d_next, f_next, s_next, n_next

    for t in range(tiles):
        d_back = diff(t, lo - 2)
        d_here = diff(t, lo - 1)
        f_here, s_here = flux(t, lo - 1)
        n_here = sensor(t, lo - 1)
        h, d_next, f_next, s_next, n_next = face(t, lo - 1, d_back, d_here, f_here, s_here, n_here)

        def body(r, carry, t=t):
            h_back, d_back, d_here, f_here, s_here, n_here = carry
            h, d_next, f_next, s_next, n_next = face(t, r, d_back, d_here, f_here, s_here, n_here)
            for c in range(4):
                d_ref[t, c, r] = h[c] - h_back[c]
            return h, d_here, d_next, f_next, s_next, n_next

        loop(lo, hi, unroll, body, (h, d_here, d_next, f_next, s_next, n_next))


def lane_flux(w, press, q):
    return [w[2], w[1] * q, w[2] * q + press, (w[3] + press) * q]


def along_lanes_fine(w_ref, p_ref, d_ref, lo, hi, ahead, emit, unroll):
    def body(r, carry):
        we, wo = ([w_ref[t, c, r] for c in range(4)] for t in range(2))
        (pe, po), (qe, qo) = ([p_ref[t, i, r] for t in range(2)] for i in (0, 2))
        se, so = jnp.abs(qe) + p_ref[0, 3, r], jnp.abs(qo) + p_ref[1, 3, r]
        pe1, po1, pom = ahead(pe, 1), ahead(po, 1), ahead(po, -1)
        qe1, se1 = ahead(qe, 1), ahead(se, 1)
        we1 = [ahead(v, 1) for v in we]
        wo1 = [ahead(v, 1) for v in wo]
        wom = [ahead(v, -1) for v in wo]
        ne = quarter_sensor(pom, pe, po)
        no = quarter_sensor(pe, po, pe1)
        ne1 = quarter_sensor(po, pe1, po1)
        ae, be = face_coefs(ne, no, se, so)
        ao, bo = face_coefs(no, ne1, so, se1)
        fe, fo, fe1 = lane_flux(we, pe, qe), lane_flux(wo, po, qo), lane_flux(we1, pe1, qe1)
        out = []
        for c in range(4):
            de = wo[c] - we[c]
            do = we1[c] - wo[c]
            he = fe[c] + fo[c] - ae * de + be * (do + (we[c] - wom[c]))
            ho = fo[c] + fe1[c] - ao * do + bo * ((wo1[c] - we1[c]) + de)
            out.append([he - ahead(ho, -1) + d_ref[0, c, r], ho - he + d_ref[1, c, r]])
        for t, w in enumerate((we, wo)):
            emit(t, r, w, [out[c][t] for c in range(4)])
        return carry

    loop(lo, hi, unroll, body)


def along_lanes_coarse(w_ref, p_ref, d_ref, lo, hi, ahead, emit, unroll):
    def body(r, carry):
        w = [w_ref[0, c, r] for c in range(4)]
        press, q = p_ref[0, 0, r], p_ref[0, 2, r]
        spec = jnp.abs(q) + p_ref[0, 3, r]
        pm, p1, p2 = ahead(press, -1), ahead(press, 1), ahead(press, 2)
        q1, s1 = ahead(q, 1), ahead(spec, 1)
        wm, w1, w2 = ([ahead(v, k) for v in w] for k in (-1, 1, 2))
        ca, cb = face_coefs(quarter_sensor(pm, press, p1), quarter_sensor(press, p1, p2), spec, s1)
        f, f1 = lane_flux(w, press, q), lane_flux(w1, p1, q1)
        out = []
        for c in range(4):
            h = f[c] + f1[c] - ca * (w1[c] - w[c]) + cb * ((w2[c] - w1[c]) + (w[c] - wm[c]))
            out.append(h - ahead(h, -1) + d_ref[0, c, r])
        emit(0, r, w, out)
        return carry

    loop(lo, hi, unroll, body)


def with_source(w, total, both, far, winf, half_h):
    out = []
    for c in range(4):
        base = total[c] if half_h == 1.0 else half_h * total[c]
        term = (both if c in (1, 2) else far) * w[c]
        if not (isinstance(winf[c], float) and winf[c] == 0.0):
            term = term - far * winf[c]
        out.append(base + term)
    return out


def weights(kind):
    far = jnp.where(kind == 2.0, 1.0, 0.0)
    return jnp.where(kind == 1.0, 2.0, far), far


def spectral_sum(p_ref, t, r):
    return jnp.abs(p_ref[t, 1, r]) + jnp.abs(p_ref[t, 2, r]) + 2.0 * p_ref[t, 3, r]


def leg(refs, ahead, winf, rows, refresh, offset):
    w, pr, dx, sm, fr, cs, cpr, cdx, csum, kk, seg, forc, corr, share = refs
    (p1, s1, p2, s2, c_state, c_seg, c_prim, c_out) = rows

    def smooth(t, r, mine, total):
        both, far = weights(w[t, 4, r])
        res = with_source(mine, total, both, far, winf(), 0.5)
        scale = 0.4 / spectral_sum(pr, t, r)
        for c in range(4):
            sm[t, c, r] = mine[c] - scale * res[c]

    def fine(t, r, mine, total):
        both, far = weights(w[t, 4, r])
        res = with_source(mine, total, both, far, winf(), 0.5)
        for c in range(4):
            fr[t, c, r] = res[c]

    primitives(w, pr, 2, *p1)
    along_rows(w, pr, dx, 2, *s1, ROW_UNROLL)
    yield "rows"
    along_lanes_fine(w, pr, dx, *s1, ahead, smooth, FINE_UNROLL)
    refresh(sm)
    yield "smoothed"
    primitives(sm, pr, 2, *p2)
    along_rows(sm, pr, dx, 2, *s2, ROW_UNROLL)
    along_lanes_fine(sm, pr, dx, *s2, ahead, fine, FINE_UNROLL)
    yield "fine"

    def four(get, k):
        i = 2 * k + offset
        return (get(0, i) + get(0, i + 1)) + (get(1, i) + get(1, i + 1))

    def state(k, carry):
        for c in range(4):
            cs[0, c, k] = 0.25 * four(lambda t, i: sm[t, c, i], k)
        return carry

    loop(*c_state, 4, state)
    refresh(cs)

    def sums(k, carry):
        for c in range(4):
            csum[0, c, k] = four(lambda t, i: fr[t, c, i], k)
        for j in range(2):
            share[0, j, k] = four(lambda t, i: weights(w[t, 4, i])[j], k)
        return carry

    loop(*c_seg, 4, sums)
    primitives(cs, cpr, 1, *c_prim)

    def segment(k, carry):
        scale = 0.2 / spectral_sum(cpr, 0, k)
        kk[0, k] = scale
        for c in range(4):
            seg[0, c, k] = cs[0, c, k] - scale * csum[0, c, k]
        return carry

    loop(*c_seg, 4, segment)
    refresh(seg)

    def coarse_residual(k, mine, total):
        return with_source(mine, total, share[0, 0, k], share[0, 1, k], winf(), 1.0)

    def force(t, k, mine, total):
        res = coarse_residual(k, mine, total)
        for c in range(4):
            forc[0, c, k] = csum[0, c, k] - res[c]

    along_rows(cs, cpr, cdx, 1, *c_out, ROW_UNROLL)
    along_lanes_coarse(cs, cpr, cdx, *c_out, ahead, force, COARSE_UNROLL)
    primitives(seg, cpr, 1, *c_prim)

    def final(t, k, mine, total):
        res = coarse_residual(k, mine, total)
        for c in range(4):
            corr[0, c, k] = -kk[0, k] * (res[c] + forc[0, c, k])

    along_rows(seg, cpr, cdx, 1, *c_out, ROW_UNROLL)
    along_lanes_coarse(seg, cpr, cdx, *c_out, ahead, final, COARSE_UNROLL)
    yield "done"


MAIN_ROWS = ((0, 36), (2, 34), (0, 36), (2, 34), (2, 18), (2, 18), (0, 20), (2, 18))
STRIP_ROWS = ((0, 24), (2, 22), (2, 22), (4, 20), (2, 10), (2, 10), (2, 10), (4, 8))


def winf_main():
    return (1.0, 0.5, 0.0, ENERGY)


def winf_strip():
    column = sub_index() <= RIGHT
    return (1.0, jnp.where(column, 0.0, 0.5), jnp.where(column, 0.5, 0.0), ENERGY)


def refresh_main(ref):
    depth = ref.shape[2]
    for t in range(ref.shape[0]):
        for c in range(4):
            for i in range(2):
                ref[t, c, i] = sub_roll(ref[t, c, depth - 4 + i], 1)
                ref[t, c, depth - 2 + i] = sub_roll(ref[t, c, 2 + i], -1)


def no_refresh(ref):
    pass


def run_to(steps, name):
    for reached in steps:
        if reached == name:
            return


def kernel(nx, ny, flow_hbm, kind_hbm, out_new, out_res, raw, raw_kind, nat, nat_kind, columns, pack, got, col_in,
           col_turned, *rest):
    main_refs, strip_refs, sems = rest[:14], rest[14:28], rest[28:]
    load_sem, copy_sem, send_sem, recv_sem = sems
    gx, gy = lax.axis_index("gx"), lax.axis_index("gy")
    up, down = lax.rem(gx + nx - 1, nx), lax.rem(gx + 1, nx)
    left, right = lax.rem(gy + ny - 1, ny), lax.rem(gy + 1, ny)
    neighbours = [(up, gy), (down, gy), (gx, left), (gx, right), (up, left), (up, right), (down, left), (down, right)]
    barrier = pltpu.get_barrier_semaphore()
    for where in neighbours:
        pl.semaphore_signal(barrier, inc=1, device_id=where, device_id_type=MESH)

    loads = []

    def load(src, dst):
        copy = pltpu.make_async_copy(src, dst, load_sem.at[len(loads)])
        copy.start()
        loads.append(copy)

    for t in range(2):
        cols = pl.ds(t * LANES, LANES)
        for s in range(SUB):
            rows = pl.ds(ROWS * s, ROWS)
            load(flow_hbm.at[:, rows, cols], raw.at[t, :, :, s, :])
            load(kind_hbm.at[rows, cols], raw_kind.at[t, :, s, :])
    first_natural = len(loads)
    for t in range(2):
        cols = pl.ds(t * LANES, LANES)
        load(flow_hbm.at[:, :, cols], nat.at[t])
        load(kind_hbm.at[:, cols], nat_kind.at[t])
    for copy in loads[:first_natural]:
        copy.wait()

    w_main, w_strip = main_refs[0], strip_refs[0]
    lane = lane_index()

    def part(r, carry):
        lane = lane_index()
        low = lane < LANES // 2
        for c in range(5):
            a, b = (raw_kind[t, r].astype(jnp.float32) if c == 4 else raw[t, c, r] for t in range(2))
            for t in range(2):
                index = jnp.bitwise_and(2 * lane + t, LANES - 1)
                w_main[t, c, r + 2] = jnp.where(low, take(a, index), take(b, index))
        return carry

    loop(0, ROWS, 4, part)
    for copy in loads[first_natural:]:
        copy.wait()

    for side in range(2):
        for i, row in enumerate((0, 248)):
            rows = pl.ds(row, 8)
            total = None
            for c in range(5):
                v = nat_kind[side, rows, :].astype(jnp.float32) if c == 4 else nat[side, c, rows, :]
                if side:
                    v = pltpu.roll(v, -8 * c % LANES, 1)
                    total = v if c == 0 else jnp.where(lane < LANES - 8 * c, v, total)
                else:
                    v = pltpu.roll(v, 8 * c, 1)
                    total = v if c == 0 else jnp.where(lane >= 8 * c, v, total)
            pack[side, i] = total

    for c, source in enumerate((0, 2, 1, 3, 4)):
        for side in range(2):
            for t in range(2):
                rows = pl.ds(t, LANES, stride=2)
                v = nat_kind[side, rows, :].astype(jnp.float32) if c == 4 else nat[side, source, rows, :]
                turned = v.T
                columns[side, t, c] = turned[112:128] if side else turned[0:16]

    refresh_main(w_main)
    pl.semaphore_wait(barrier, 8)
    number = 0
    copies = []

    def send(src, dst, where):
        nonlocal number
        copy = pltpu.make_async_remote_copy(
            src_ref=src, dst_ref=dst, send_sem=send_sem.at[number], recv_sem=recv_sem.at[number],
            device_id=where, device_id_type=MESH)
        copy.start()
        copies.append(copy)
        number += 1

    def strip_at(first, count, sub):
        return w_strip.at[:, :, pl.ds(first, count), sub, :]

    send(w_main.at[:, :, pl.ds(26, 8), 7, :], strip_at(0, 8, TOP), (down, gy))
    send(w_main.at[:, :, pl.ds(2, 8), 0, :], strip_at(16, 8, BOT), (up, gy))
    send(pack.at[1, 1], got.at[0], (down, right))
    send(pack.at[0, 1], got.at[1], (down, left))
    send(pack.at[1, 0], got.at[2], (up, right))
    send(pack.at[0, 0], got.at[3], (up, left))
    top, bottom = w_main.at[:, :, pl.ds(2, 16), 0, :], w_main.at[:, :, pl.ds(18, 16), 7, :]
    send(top, strip_at(8, 16, TOP_L), (gx, right))
    send(top, strip_at(8, 16, TOP_R), (gx, left))
    send(bottom, strip_at(0, 16, BOT_L), (gx, right))
    send(bottom, strip_at(0, 16, BOT_R), (gx, left))
    send(columns.at[1, :, :, pl.ds(8, 8), :], strip_at(0, 8, LEFT), (gx, right))
    send(columns.at[0, :, :, pl.ds(0, 8), :], strip_at(16, 8, RIGHT), (gx, left))

    own = []
    for src, dst in (
        (top, strip_at(8, 16, TOP)),
        (bottom, strip_at(0, 16, BOT)),
        (columns.at[0], strip_at(8, 16, LEFT)),
        (columns.at[1], strip_at(0, 16, RIGHT)),
    ):
        copy = pltpu.make_async_copy(src, dst, copy_sem.at[len(own)])
        copy.start()
        own.append(copy)

    run_to(leg(main_refs, ahead_main, winf_main, MAIN_ROWS, refresh_main, -2), "done")

    for copy in own:
        copy.wait()
    for copy in copies:
        copy.wait_recv()

    def corners(r, carry):
        sub, lane = sub_index(), lane_index()
        total = jnp.zeros((SUB, LANES), jnp.float32)
        for k, where in enumerate((TOP_L, TOP_R, BOT_L, BOT_R)):
            total = jnp.where(sub == where, jnp.broadcast_to(got[k, pl.ds(r, 1), :], (SUB, LANES)), total)
        at_top = jnp.logical_or(sub == TOP_L, sub == TOP_R)
        at_bottom = jnp.logical_or(sub == BOT_L, sub == BOT_R)
        for t in range(2):
            for c in range(5):
                from_left = 120 - 8 * c + 2 * (lane - 124) + t
                from_right = 8 * c + 2 * lane + t
                index = jnp.where(lane >= 124, from_left, jnp.where(lane < 4, from_right, 0))
                v = take(total, index)
                w_strip[t, c, r] = jnp.where(at_top, v, w_strip[t, c, r])
                w_strip[t, c, r + 16] = jnp.where(at_bottom, v, w_strip[t, c, r + 16])
        return carry

    loop(0, 8, 4, corners)
    run_to(leg(strip_refs, ahead_strip, winf_strip, STRIP_ROWS, no_refresh, 0), "done")

    sm_main, fr_main, corr_main = main_refs[3], main_refs[4], main_refs[12]
    sm_strip, fr_strip, corr_strip = strip_refs[3], strip_refs[4], strip_refs[12]

    def gather_columns(i, carry):
        for t in range(2):
            for c, target in enumerate((0, 2, 1, 3)):
                v = sm_strip[t, c, i + 8] + corr_strip[0, c, (i + 8) // 2]
                col_in[t, pl.ds(target * 8 + i, 2, stride=64), :] = v[0:2]
                v = fr_strip[t, c, i + 8]
                col_in[t, pl.ds((target + 4) * 8 + i, 2, stride=64), :] = v[0:2]
        return carry

    loop(0, 8, 2, gather_columns)
    for t in range(2):
        col_turned[t] = col_in[t].T

    def finish(edge):
        def body(k, carry):
            lane, sub = lane_index(), sub_index()
            at_side = jnp.logical_or(lane < 4, lane >= 124)
            even = lane % 2 == 0
            half = lane // 2
            for i in range(2):
                r = 2 * k + i
                side = col_turned[i, pl.ds(k, SUB, stride=16), :]
                for a in range(8):
                    out, c = (out_new, a) if a < 4 else (out_res, a - 4)
                    pair = []
                    for t in range(2):
                        if a < 4:
                            v = sm_main[t, c, r + 2] + corr_main[0, c, k + 2]
                        else:
                            v = fr_main[t, c, r + 2]
                        index = 8 * a + t + 2 * jnp.where(lane < 4, lane, jnp.where(lane >= 124, lane - 92, 0))
                        v = jnp.where(at_side, take(side, index), v)
                        if edge is not None:
                            at, where, first, coarse_first = edge
                            j = r + first
                            s = fr_strip[t, c, j] if a >= 4 else sm_strip[t, c, j] + corr_strip[0, c, k + coarse_first]
                            v = jnp.where(sub == at, sub_roll(s, at - where), v)
                        pair.append(v)
                    for tile in range(2):
                        x, y = (take(v, half + 64 * tile) for v in pair)
                        out[tile, c, r] = jnp.where(even, x, y)
            return carry

        return body

    loop(0, 4, 1, finish((0, TOP, 8, 4)))
    loop(4, 12, 1, finish(None))
    loop(12, 16, 1, finish((7, BOT, -16, -8)))
    for copy in copies:
        copy.wait_send()


def put_kernel(new, res, new_hbm, res_hbm, sems):
    copies = []
    for src, dst in ((new, new_hbm), (res, res_hbm)):
        for t in range(2):
            for s in range(SUB):
                copy = pltpu.make_async_copy(
                    src.at[t, :, :, s, :], dst.at[:, pl.ds(ROWS * s, ROWS), pl.ds(t * LANES, LANES)], sems.at[len(copies)])
                copy.start()
                copies.append(copy)
    for copy in copies:
        copy.wait()


def vmem(*shape):
    return pltpu.VMEM(shape, jnp.float32)


def domain(rows, coarse_rows):
    tile = (SUB, LANES)
    return [
        vmem(2, 5, rows, *tile),
        vmem(2, 4, rows, *tile),
        vmem(2, 4, rows, *tile),
        vmem(2, 4, rows, *tile),
        vmem(2, 4, rows, *tile),
        vmem(1, 4, coarse_rows, *tile),
        vmem(1, 4, coarse_rows, *tile),
        vmem(1, 4, coarse_rows, *tile),
        vmem(1, 4, coarse_rows, *tile),
        vmem(1, coarse_rows, *tile),
        vmem(1, 4, coarse_rows, *tile),
        vmem(1, 4, coarse_rows, *tile),
        vmem(1, 4, coarse_rows, *tile),
        vmem(1, 2, coarse_rows, *tile),
    ]


def solution(mesh):
    nx, ny = mesh.shape["gx"], mesh.shape["gy"]

    def local(flow_state, cell_kind):
        hbm = pl.BlockSpec(memory_space=pl.ANY)
        held = pl.BlockSpec(memory_space=pltpu.VMEM)
        block = (2, 4, ROWS, SUB, LANES)
        new, res = pl.pallas_call(
            functools.partial(kernel, nx, ny),
            out_shape=(vmem(*block), vmem(*block)),
            in_specs=[hbm, hbm],
            out_specs=(held, held),
            scratch_shapes=[
                vmem(*block),
                pltpu.VMEM((2, ROWS, SUB, LANES), jnp.int32),
                vmem(2, 4, 256, LANES),
                pltpu.VMEM((2, 256, LANES), jnp.int32),
                vmem(2, 2, 5, 16, LANES),
                vmem(2, 2, 8, LANES),
                vmem(4, 8, LANES),
                vmem(2, LANES, LANES),
                vmem(2, LANES, LANES),
                *domain(36, 20),
                *domain(24, 12),
                pltpu.SemaphoreType.DMA((36,)),
                pltpu.SemaphoreType.DMA((4,)),
                pltpu.SemaphoreType.DMA((12,)),
                pltpu.SemaphoreType.DMA((12,)),
            ],
            compiler_params=pltpu.CompilerParams(
                collective_id=0, has_side_effects=True, vmem_limit_bytes=64_900_000
            ),
        )(flow_state, cell_kind)
        out = jax.ShapeDtypeStruct(flow_state.shape, jnp.float32)
        return pl.pallas_call(
            put_kernel,
            out_shape=(out, out),
            in_specs=[hbm, hbm],
            out_specs=(hbm, hbm),
            scratch_shapes=[pltpu.SemaphoreType.DMA((32,))],
            compiler_params=pltpu.CompilerParams(vmem_limit_bytes=1 << 20),
        )(new, res)

    return jax.shard_map(
        local,
        mesh=mesh,
        in_specs=(P(None, "gx", "gy"), P("gx", "gy")),
        out_specs=(P(None, "gx", "gy"), P(None, "gx", "gy")),
        check_vma=False,
    )
```

```python
import functools

import jax
import jax.numpy as jnp
from jax import lax
from jax.experimental import pallas as pl
from jax.experimental.pallas import tpu as pltpu
from jax.sharding import PartitionSpec as P

MESH = pl.DeviceIdType.MESH
LANES = 128
SUB = 8
ROWS = 32
STRIP = 24

ENERGY = 1.0 / 0.56 + 0.125

LEFT, RIGHT, TOP_L, TOP, TOP_R, BOT_L, BOT, BOT_R = range(8)

FINE_UNROLL = 4
ROW_UNROLL = 8
COARSE_UNROLL = 4


def lane_index():
    return lax.broadcasted_iota(jnp.int32, (SUB, LANES), 1)


def sub_index():
    return lax.broadcasted_iota(jnp.int32, (SUB, LANES), 0)


def sub_roll(v, shift):
    return pltpu.roll(v, shift % SUB, 0)


def take(v, index):
    return jnp.take_along_axis(v, index, axis=1)


def ahead_main(v, k):
    return pltpu.roll(v, -k % LANES, 1)


def ahead_strip(v, k):
    here = pltpu.roll(v, -k % LANES, 1)
    lane = lane_index()
    if k > 0:
        return jnp.where(lane >= LANES - k, sub_roll(here, -1), here)
    return jnp.where(lane < -k, sub_roll(here, 1), here)


def loop(lo, hi, unroll, body, carry=0):
    count = hi - lo
    while count % unroll:
        unroll -= 1

    def run(step, carry):
        for i in range(unroll):
            carry = body(lo + step * unroll + i, carry)
        return carry

    return lax.fori_loop(0, count // unroll, run, carry)


def primitives(w_ref, p_ref, tiles, lo, hi, unroll=4):
    def body(r, carry):
        for t in range(tiles):
            density, mom_r, mom_l, energy = (w_ref[t, c, r] for c in range(4))
            inverse = 1.0 / density
            u = mom_r * inverse
            v = mom_l * inverse
            press = 0.4 * (energy - 0.5 * (mom_r * u + mom_l * v))
            p_ref[t, 0, r] = press
            p_ref[t, 1, r] = u
            p_ref[t, 2, r] = v
            p_ref[t, 3, r] = jnp.sqrt(1.4 * press * inverse)
        return carry

    loop(lo, hi, unroll, body)


def face_coefs(sensor_a, sensor_b, spec_a, spec_b):
    second = jnp.maximum(sensor_a, sensor_b)
    fourth = jnp.maximum(0.0, 1.0 / 32.0 - second)
    total = spec_a + spec_b
    coef_b = total * fourth
    coef_a = total * second + 2.0 * coef_b
    return coef_a, coef_b


def quarter_sensor(low, mid, high):
    ends = low + high
    twice = 2.0 * mid
    return 0.25 * jnp.abs(ends - twice) / (ends + twice)


def along_rows(w_ref, p_ref, d_ref, tiles, lo, hi, unroll):
    def flux(t, r):
        w = [w_ref[t, c, r] for c in range(4)]
        press, q, sound = p_ref[t, 0, r], p_ref[t, 1, r], p_ref[t, 3, r]
        f = [w[1], w[1] * q + press, w[2] * q, (w[3] + press) * q]
        return f, jnp.abs(q) + sound

    def sensor(t, r):
        return quarter_sensor(p_ref[t, 0, r - 1], p_ref[t, 0, r], p_ref[t, 0, r + 1])

    def diff(t, r):
        return [w_ref[t, c, r + 1] - w_ref[t, c, r] for c in range(4)]

    def face(t, r, d_back, d_here, f_here, s_here, n_here):
        d_next = diff(t, r + 1)
        f_next, s_next = flux(t, r + 1)
        n_next = sensor(t, r + 1)
        ca, cb = face_coefs(n_here, n_next, s_here, s_next)
        h = [
            f_here[c] + f_next[c] - ca * d_here[c] + cb * (d_next[c] + d_back[c])
            for c in range(4)
        ]
        return h, d_next, f_next, s_next, n_next

    for t in range(tiles):
        d_back = diff(t, lo - 2)
        d_here = diff(t, lo - 1)
        f_here, s_here = flux(t, lo - 1)
        n_here = sensor(t, lo - 1)
        h, d_next, f_next, s_next, n_next = face(t, lo - 1, d_back, d_here, f_here, s_here, n_here)

        def body(r, carry, t=t):
            h_back, d_back, d_here, f_here, s_here, n_here = carry
            h, d_next, f_next, s_next, n_next = face(t, r, d_back, d_here, f_here, s_here, n_here)
            for c in range(4):
                d_ref[t, c, r] = h[c] - h_back[c]
            return h, d_here, d_next, f_next, s_next, n_next

        loop(lo, hi, unroll, body, (h, d_here, d_next, f_next, s_next, n_next))


def lane_flux(w, press, q):
    return [w[2], w[1] * q, w[2] * q + press, (w[3] + press) * q]


def along_lanes_fine(w_ref, p_ref, d_ref, lo, hi, ahead, emit, unroll):
    def body(r, carry):
        we, wo = ([w_ref[t, c, r] for c in range(4)] for t in range(2))
        (pe, po), (qe, qo) = ([p_ref[t, i, r] for t in range(2)] for i in (0, 2))
        se, so = jnp.abs(qe) + p_ref[0, 3, r], jnp.abs(qo) + p_ref[1, 3, r]
        pe1, po1, pom = ahead(pe, 1), ahead(po, 1), ahead(po, -1)
        qe1, se1 = ahead(qe, 1), ahead(se, 1)
        we1 = [ahead(v, 1) for v in we]
        wo1 = [ahead(v, 1) for v in wo]
        wom = [ahead(v, -1) for v in wo]
        ne = quarter_sensor(pom, pe, po)
        no = quarter_sensor(pe, po, pe1)
        ne1 = quarter_sensor(po, pe1, po1)
        ae, be = face_coefs(ne, no, se, so)
        ao, bo = face_coefs(no, ne1, so, se1)
        fe, fo, fe1 = lane_flux(we, pe, qe), lane_flux(wo, po, qo), lane_flux(we1, pe1, qe1)
        out = []
        for c in range(4):
            de = wo[c] - we[c]
            do = we1[c] - wo[c]
            he = fe[c] + fo[c] - ae * de + be * (do + (we[c] - wom[c]))
            ho = fo[c] + fe1[c] - ao * do + bo * ((wo1[c] - we1[c]) + de)
            out.append([he - ahead(ho, -1) + d_ref[0, c, r], ho - he + d_ref[1, c, r]])
        for t, w in enumerate((we, wo)):
            emit(t, r, w, [out[c][t] for c in range(4)])
        return carry

    loop(lo, hi, unroll, body)


def along_lanes_coarse(w_ref, p_ref, d_ref, lo, hi, ahead, emit, unroll):
    def body(r, carry):
        w = [w_ref[0, c, r] for c in range(4)]
        press, q = p_ref[0, 0, r], p_ref[0, 2, r]
        spec = jnp.abs(q) + p_ref[0, 3, r]
        pm, p1, p2 = ahead(press, -1), ahead(press, 1), ahead(press, 2)
        q1, s1 = ahead(q, 1), ahead(spec, 1)
        wm, w1, w2 = ([ahead(v, k) for v in w] for k in (-1, 1, 2))
        ca, cb = face_coefs(quarter_sensor(pm, press, p1), quarter_sensor(press, p1, p2), spec, s1)
        f, f1 = lane_flux(w, press, q), lane_flux(w1, p1, q1)
        out = []
        for c in range(4):
            h = f[c] + f1[c] - ca * (w1[c] - w[c]) + cb * ((w2[c] - w1[c]) + (w[c] - wm[c]))
            out.append(h - ahead(h, -1) + d_ref[0, c, r])
        emit(0, r, w, out)
        return carry

    loop(lo, hi, unroll, body)


def with_source(w, total, both, far, winf, half_h):
    out = []
    for c in range(4):
        base = total[c] if half_h == 1.0 else half_h * total[c]
        term = (both if c in (1, 2) else far) * w[c]
        if not (isinstance(winf[c], float) and winf[c] == 0.0):
            term = term - far * winf[c]
        out.append(base + term)
    return out


def weights(kind):
    far = jnp.where(kind == 2.0, 1.0, 0.0)
    return jnp.where(kind == 1.0, 2.0, far), far


def spectral_sum(p_ref, t, r):
    return jnp.abs(p_ref[t, 1, r]) + jnp.abs(p_ref[t, 2, r]) + 2.0 * p_ref[t, 3, r]


def leg(refs, ahead, winf, rows, refresh, offset):
    w, pr, dx, sm, fr, cs, cpr, cdx, csum, kk, seg, forc, corr, share = refs
    (p1, s1, p2, s2, c_state, c_seg, c_prim, c_out) = rows

    def smooth(t, r, mine, total):
        both, far = weights(w[t, 4, r])
        res = with_source(mine, total, both, far, winf(), 0.5)
        scale = 0.4 / spectral_sum(pr, t, r)
        for c in range(4):
            sm[t, c, r] = mine[c] - scale * res[c]

    def fine(t, r, mine, total):
        both, far = weights(w[t, 4, r])
        res = with_source(mine, total, both, far, winf(), 0.5)
        for c in range(4):
            fr[t, c, r] = res[c]

    primitives(w, pr, 2, *p1)
    along_rows(w, pr, dx, 2, *s1, ROW_UNROLL)
    yield "rows"
    along_lanes_fine(w, pr, dx, *s1, ahead, smooth, FINE_UNROLL)
    refresh(sm)
    yield "smoothed"
    primitives(sm, pr, 2, *p2)
    along_rows(sm, pr, dx, 2, *s2, ROW_UNROLL)
    along_lanes_fine(sm, pr, dx, *s2, ahead, fine, FINE_UNROLL)
    yield "fine"

    def four(get, k):
        i = 2 * k + offset
        return (get(0, i) + get(0, i + 1)) + (get(1, i) + get(1, i + 1))

    def state(k, carry):
        for c in range(4):
            cs[0, c, k] = 0.25 * four(lambda t, i: sm[t, c, i], k)
        return carry

    loop(*c_state, 4, state)
    refresh(cs)

    def sums(k, carry):
        for c in range(4):
            csum[0, c, k] = four(lambda t, i: fr[t, c, i], k)
        for j in range(2):
            share[0, j, k] = four(lambda t, i: weights(w[t, 4, i])[j], k)
        return carry

    loop(*c_seg, 4, sums)
    primitives(cs, cpr, 1, *c_prim)

    def segment(k, carry):
        scale = 0.2 / spectral_sum(cpr, 0, k)
        kk[0, k] = scale
        for c in range(4):
            seg[0, c, k] = cs[0, c, k] - scale * csum[0, c, k]
        return carry

    loop(*c_seg, 4, segment)
    refresh(seg)

    def coarse_residual(k, mine, total):
        return with_source(mine, total, share[0, 0, k], share[0, 1, k], winf(), 1.0)

    def force(t, k, mine, total):
        res = coarse_residual(k, mine, total)
        for c in range(4):
            forc[0, c, k] = csum[0, c, k] - res[c]

    along_rows(cs, cpr, cdx, 1, *c_out, ROW_UNROLL)
    along_lanes_coarse(cs, cpr, cdx, *c_out, ahead, force, COARSE_UNROLL)
    primitives(seg, cpr, 1, *c_prim)

    def final(t, k, mine, total):
        res = coarse_residual(k, mine, total)
        for c in range(4):
            corr[0, c, k] = -kk[0, k] * (res[c] + forc[0, c, k])

    along_rows(seg, cpr, cdx, 1, *c_out, ROW_UNROLL)
    along_lanes_coarse(seg, cpr, cdx, *c_out, ahead, final, COARSE_UNROLL)
    yield "done"


MAIN_ROWS = ((0, 36), (2, 34), (0, 36), (2, 34), (2, 18), (2, 18), (0, 20), (2, 18))
STRIP_ROWS = ((0, 24), (2, 22), (2, 22), (4, 20), (2, 10), (2, 10), (2, 10), (4, 8))


def winf_main():
    return (1.0, 0.5, 0.0, ENERGY)


def winf_strip():
    column = sub_index() <= RIGHT
    return (1.0, jnp.where(column, 0.0, 0.5), jnp.where(column, 0.5, 0.0), ENERGY)


def refresh_main(ref):
    depth = ref.shape[2]
    for t in range(ref.shape[0]):
        for c in range(4):
            for i in range(2):
                ref[t, c, i] = sub_roll(ref[t, c, depth - 4 + i], 1)
                ref[t, c, depth - 2 + i] = sub_roll(ref[t, c, 2 + i], -1)


def no_refresh(ref):
    pass


def run_to(steps, name):
    for reached in steps:
        if reached == name:
            return


def kernel(nx, ny, flow_hbm, kind_hbm, out_new, out_res, raw, raw_kind, nat, nat_kind, columns, pack, got, col_in,
           col_turned, whole, *rest):
    main_refs, strip_refs, sems = rest[:14], rest[14:28], rest[28:]
    load_sem, copy_sem, send_sem, recv_sem = sems
    gx, gy = lax.axis_index("gx"), lax.axis_index("gy")
    up, down = lax.rem(gx + nx - 1, nx), lax.rem(gx + 1, nx)
    left, right = lax.rem(gy + ny - 1, ny), lax.rem(gy + 1, ny)
    neighbours = [(up, gy), (down, gy), (gx, left), (gx, right), (up, left), (up, right), (down, left), (down, right)]
    barrier = pltpu.get_barrier_semaphore()
    for where in neighbours:
        pl.semaphore_signal(barrier, inc=1, device_id=where, device_id_type=MESH)

    loads = []

    def load(src, dst):
        copy = pltpu.make_async_copy(src, dst, load_sem.at[len(loads)])
        copy.start()
        loads.append(copy)

    for t in range(2):
        cols = pl.ds(t * LANES, LANES)
        for s in range(SUB):
            rows = pl.ds(ROWS * s, ROWS)
            load(flow_hbm.at[:, rows, cols], raw.at[t, :, :, s, :])
            load(kind_hbm.at[rows, cols], raw_kind.at[t, :, s, :])
    first_natural = len(loads)
    for t in range(2):
        cols = pl.ds(t * LANES, LANES)
        load(flow_hbm.at[:, :, cols], nat.at[t])
        load(kind_hbm.at[:, cols], nat_kind.at[t])
    for copy in loads[:first_natural]:
        copy.wait()

    w_main, w_strip = main_refs[0], strip_refs[0]
    lane = lane_index()

    for t in range(2):
        low = lane < LANES // 2
        index = jnp.bitwise_and(2 * lane + t, LANES - 1)

        def part(r, carry):
            for c in range(5):
                a, b = (raw_kind[s, r].astype(jnp.float32) if c == 4 else raw[s, c, r] for s in range(2))
                w_main[t, c, r + 2] = jnp.where(low, take(a, index), take(b, index))
            return carry

        loop(0, ROWS, 8, part)
    for copy in loads[first_natural:]:
        copy.wait()

    for side in range(2):
        for i, row in enumerate((0, 248)):
            rows = pl.ds(row, 8)
            total = None
            for c in range(5):
                v = nat_kind[side, rows, :].astype(jnp.float32) if c == 4 else nat[side, c, rows, :]
                v = pltpu.roll(v, 8 * (c + side), 1)
                total = v if c == 0 else jnp.where(lane >= 8 * c, v, total)
            group = lane // 8
            pack[side, i] = take(total, 8 * (group // 2) + 2 * (lane % 4) + group % 2)

    for c, source in enumerate((0, 2, 1, 3, 4)):
        for side in range(2):
            for t in range(2):
                rows = pl.ds(t, LANES, stride=2)
                v = nat_kind[side, rows, :].astype(jnp.float32) if c == 4 else nat[side, source, rows, :]
                turned = v.T
                columns[side, t, c] = turned[112:128] if side else turned[0:16]

    refresh_main(w_main)
    pl.semaphore_wait(barrier, 8)
    number = 0
    copies = []

    def send(src, dst, where):
        nonlocal number
        copy = pltpu.make_async_remote_copy(
            src_ref=src, dst_ref=dst, send_sem=send_sem.at[number], recv_sem=recv_sem.at[number],
            device_id=where, device_id_type=MESH)
        copy.start()
        copies.append(copy)
        number += 1

    def strip_at(first, count, sub):
        return w_strip.at[:, :, pl.ds(first, count), sub, :]

    send(w_main.at[:, :, pl.ds(26, 8), 7, :], strip_at(0, 8, TOP), (down, gy))
    send(w_main.at[:, :, pl.ds(2, 8), 0, :], strip_at(16, 8, BOT), (up, gy))
    send(pack.at[1, 1], got.at[0], (down, right))
    send(pack.at[0, 1], got.at[1], (down, left))
    send(pack.at[1, 0], got.at[2], (up, right))
    send(pack.at[0, 0], got.at[3], (up, left))
    top, bottom = w_main.at[:, :, pl.ds(2, 16), 0, :], w_main.at[:, :, pl.ds(18, 16), 7, :]
    send(top, strip_at(8, 16, TOP_L), (gx, right))
    send(top, strip_at(8, 16, TOP_R), (gx, left))
    send(bottom, strip_at(0, 16, BOT_L), (gx, right))
    send(bottom, strip_at(0, 16, BOT_R), (gx, left))
    send(columns.at[1, :, :, pl.ds(8, 8), :], strip_at(0, 8, LEFT), (gx, right))
    send(columns.at[0, :, :, pl.ds(0, 8), :], strip_at(16, 8, RIGHT), (gx, left))

    own = []
    for src, dst in (
        (top, strip_at(8, 16, TOP)),
        (bottom, strip_at(0, 16, BOT)),
        (columns.at[0], strip_at(8, 16, LEFT)),
        (columns.at[1], strip_at(0, 16, RIGHT)),
    ):
        copy = pltpu.make_async_copy(src, dst, copy_sem.at[len(own)])
        copy.start()
        own.append(copy)

    run_to(leg(main_refs, ahead_main, winf_main, MAIN_ROWS, refresh_main, -2), "done")

    for copy in own:
        copy.wait()
    for copy in copies:
        copy.wait_recv()

    def corners(r, carry):
        sub = sub_index()
        total = jnp.zeros((SUB, LANES), jnp.float32)
        for k, where in enumerate((TOP_L, TOP_R, BOT_L, BOT_R)):
            total = jnp.where(sub == where, jnp.broadcast_to(got[k, pl.ds(r, 1), :], (SUB, LANES)), total)
        at_top = jnp.logical_or(sub == TOP_L, sub == TOP_R)
        at_bottom = jnp.logical_or(sub == BOT_L, sub == BOT_R)
        for t in range(2):
            for c in range(5):
                v = pltpu.roll(total, -(8 * (2 * c + t) + 4) % LANES, 1)
                w_strip[t, c, r] = jnp.where(at_top, v, w_strip[t, c, r])
                w_strip[t, c, r + 16] = jnp.where(at_bottom, v, w_strip[t, c, r + 16])
        return carry

    loop(0, 8, 4, corners)
    run_to(leg(strip_refs, ahead_strip, winf_strip, STRIP_ROWS, no_refresh, 0), "done")

    sm_main, fr_main, corr_main = main_refs[3], main_refs[4], main_refs[12]
    sm_strip, fr_strip, corr_strip = strip_refs[3], strip_refs[4], strip_refs[12]

    for i in range(8):
        for t in range(2):
            for c, target in enumerate((0, 2, 1, 3)):
                for a, v in (
                    (target, sm_strip[t, c, i + 8] + corr_strip[0, c, (i + 8) // 2]),
                    (target + 4, fr_strip[t, c, i + 8]),
                ):
                    row = 8 * (2 * a + i % 2) + i // 2
                    col_in[t, pl.ds(row + 4, 1), :] = v[LEFT : LEFT + 1]
                    col_in[t, pl.ds(row, 1), :] = v[RIGHT : RIGHT + 1]
    for t in range(2):
        col_turned[t] = col_in[t].T

    def collect(edge):
        def body(k, carry):
            lane, sub = lane_index(), sub_index()
            at_side = jnp.logical_or(lane < 4, lane >= 124)
            for i in range(2):
                r = 2 * k + i
                side = col_turned[i, pl.ds(k, SUB, stride=16), :]
                for a in range(8):
                    c = a % 4
                    for t in range(2):
                        v = fr_main[t, c, r + 2] if a >= 4 else sm_main[t, c, r + 2] + corr_main[0, c, k + 2]
                        v = jnp.where(at_side, pltpu.roll(side, -(8 * (2 * a + t) + 4) % LANES, 1), v)
                        if edge is not None:
                            at, where, first, coarse_first = edge
                            j = r + first
                            s = fr_strip[t, c, j] if a >= 4 else sm_strip[t, c, j] + corr_strip[0, c, k + coarse_first]
                            v = jnp.where(sub == at, sub_roll(s, at - where), v)
                        whole[t, a, r] = v
            return carry

        return body

    loop(0, 4, 2, collect((0, TOP, 8, 4)))
    loop(4, 12, 2, collect(None))
    loop(12, 16, 2, collect((7, BOT, -16, -8)))

    for tile in range(2):
        even = lane % 2 == 0
        index = lane // 2 + 64 * tile

        def join(r, carry):
            for a in range(8):
                out, c = (out_new, a) if a < 4 else (out_res, a - 4)
                x, y = (take(whole[t, a, r], index) for t in range(2))
                out[tile, c, r] = jnp.where(even, x, y)
            return carry

        loop(0, ROWS, 4, join)
    for copy in copies:
        copy.wait_send()


def put_kernel(new, res, new_hbm, res_hbm, sems):
    copies = []
    for src, dst in ((new, new_hbm), (res, res_hbm)):
        for t in range(2):
            for s in range(SUB):
                copy = pltpu.make_async_copy(
                    src.at[t, :, :, s, :], dst.at[:, pl.ds(ROWS * s, ROWS), pl.ds(t * LANES, LANES)], sems.at[len(copies)])
                copy.start()
                copies.append(copy)
    for copy in copies:
        copy.wait()


def vmem(*shape):
    return pltpu.VMEM(shape, jnp.float32)


def domain(rows, coarse_rows):
    tile = (SUB, LANES)
    return [
        vmem(2, 5, rows, *tile),
        vmem(2, 4, rows, *tile),
        vmem(2, 4, rows, *tile),
        vmem(2, 4, rows, *tile),
        vmem(2, 4, rows, *tile),
        vmem(1, 4, coarse_rows, *tile),
        vmem(1, 4, coarse_rows, *tile),
        vmem(1, 4, coarse_rows, *tile),
        vmem(1, 4, coarse_rows, *tile),
        vmem(1, coarse_rows, *tile),
        vmem(1, 4, coarse_rows, *tile),
        vmem(1, 4, coarse_rows, *tile),
        vmem(1, 4, coarse_rows, *tile),
        vmem(1, 2, coarse_rows, *tile),
    ]


def solution(mesh):
    nx, ny = mesh.shape["gx"], mesh.shape["gy"]

    def local(flow_state, cell_kind):
        hbm = pl.BlockSpec(memory_space=pl.ANY)
        held = pl.BlockSpec(memory_space=pltpu.VMEM)
        block = (2, 4, ROWS, SUB, LANES)
        new, res = pl.pallas_call(
            functools.partial(kernel, nx, ny),
            out_shape=(vmem(*block), vmem(*block)),
            in_specs=[hbm, hbm],
            out_specs=(held, held),
            scratch_shapes=[
                vmem(*block),
                pltpu.VMEM((2, ROWS, SUB, LANES), jnp.int32),
                vmem(2, 4, 256, LANES),
                pltpu.VMEM((2, 256, LANES), jnp.int32),
                vmem(2, 2, 5, 16, LANES),
                vmem(2, 2, 8, LANES),
                vmem(4, 8, LANES),
                vmem(2, LANES, LANES),
                vmem(2, LANES, LANES),
                vmem(2, 8, ROWS, SUB, LANES),
                *domain(36, 20),
                *domain(24, 12),
                pltpu.SemaphoreType.DMA((36,)),
                pltpu.SemaphoreType.DMA((4,)),
                pltpu.SemaphoreType.DMA((12,)),
                pltpu.SemaphoreType.DMA((12,)),
            ],
            compiler_params=pltpu.CompilerParams(
                collective_id=0, has_side_effects=True, vmem_limit_bytes=64_900_000
            ),
        )(flow_state, cell_kind)
        out = jax.ShapeDtypeStruct(flow_state.shape, jnp.float32)
        return pl.pallas_call(
            put_kernel,
            out_shape=(out, out),
            in_specs=[hbm, hbm],
            out_specs=(hbm, hbm),
            scratch_shapes=[pltpu.SemaphoreType.DMA((32,))],
            compiler_params=pltpu.CompilerParams(vmem_limit_bytes=1 << 20),
        )(new, res)

    return jax.shard_map(
        local,
        mesh=mesh,
        in_specs=(P(None, "gx", "gy"), P("gx", "gy")),
        out_specs=(P(None, "gx", "gy"), P(None, "gx", "gy")),
        check_vma=False,
    )
```

```python
import functools

import jax
import jax.numpy as jnp
from jax import lax
from jax.experimental import pallas as pl
from jax.experimental.pallas import tpu as pltpu
from jax.sharding import PartitionSpec as P

MESH = pl.DeviceIdType.MESH
LANES = 128
SUB = 8
ROWS = 32
STRIP = 24

ENERGY = 1.0 / 0.56 + 0.125

LEFT, RIGHT, TOP_L, TOP, TOP_R, BOT_L, BOT, BOT_R = range(8)

FINE_UNROLL = 4
JOIN_UNROLL = 8
PART_UNROLL = 16
ROW_UNROLL = 8
COARSE_UNROLL = 4


def lane_index():
    return lax.broadcasted_iota(jnp.int32, (SUB, LANES), 1)


def sub_index():
    return lax.broadcasted_iota(jnp.int32, (SUB, LANES), 0)


def sub_roll(v, shift):
    return pltpu.roll(v, shift % SUB, 0)


def take(v, index):
    return jnp.take_along_axis(v, index, axis=1)


def ahead_main(v, k):
    return pltpu.roll(v, -k % LANES, 1)


def ahead_strip(v, k):
    here = pltpu.roll(v, -k % LANES, 1)
    lane = lane_index()
    if k > 0:
        return jnp.where(lane >= LANES - k, sub_roll(here, -1), here)
    return jnp.where(lane < -k, sub_roll(here, 1), here)


def loop(lo, hi, unroll, body, carry=0):
    count = hi - lo
    while count % unroll:
        unroll -= 1

    def run(step, carry):
        for i in range(unroll):
            carry = body(lo + step * unroll + i, carry)
        return carry

    return lax.fori_loop(0, count // unroll, run, carry)


def staged_loop(lo, hi, unroll, prepare, body):
    count = hi - lo
    while count % unroll:
        unroll -= 1
    for i in range(unroll):
        prepare(lo + i)

    def run(step, carry):
        first = lo + step * unroll
        for i in range(unroll):
            prepare(first + unroll + i)
        for i in range(unroll):
            body(first + i)
        return carry

    lax.fori_loop(0, count // unroll - 1, run, 0)
    for i in range(unroll):
        body(hi - unroll + i)


def primitives(w_ref, p_ref, tiles, lo, hi, unroll=4):
    def body(r, carry):
        for t in range(tiles):
            density, mom_r, mom_l, energy = (w_ref[t, c, r] for c in range(4))
            inverse = 1.0 / density
            u = mom_r * inverse
            v = mom_l * inverse
            press = 0.4 * (energy - 0.5 * (mom_r * u + mom_l * v))
            p_ref[t, 0, r] = press
            p_ref[t, 1, r] = u
            p_ref[t, 2, r] = v
            p_ref[t, 3, r] = jnp.sqrt(1.4 * press * inverse)
        return carry

    loop(lo, hi, unroll, body)


def face_coefs(sensor_a, sensor_b, spec_a, spec_b):
    second = jnp.maximum(sensor_a, sensor_b)
    fourth = jnp.maximum(0.0, 1.0 / 32.0 - second)
    total = spec_a + spec_b
    coef_b = total * fourth
    coef_a = total * second + 2.0 * coef_b
    return coef_a, coef_b


def quarter_sensor(low, mid, high):
    ends = low + high
    twice = 2.0 * mid
    return 0.25 * jnp.abs(ends - twice) / (ends + twice)


def shifted_fine(w_ref, p_ref, x_ref, ahead):
    def shifted(r):
        for c in range(4):
            x_ref[c, r] = ahead(w_ref[0, c, r], 1)
        for i, j in enumerate((0, 2, 3)):
            x_ref[4 + i, r] = ahead(p_ref[0, j, r], 1)
        for c in range(4):
            x_ref[7 + c, r] = ahead(w_ref[1, c, r], 1)
            x_ref[11 + c, r] = ahead(w_ref[1, c, r], -1)
        x_ref[15, r] = ahead(p_ref[1, 0, r], 1)
        x_ref[16, r] = ahead(p_ref[1, 0, r], -1)

    return shifted


def shifted_coarse(w_ref, p_ref, x_ref, ahead):
    def shifted(r):
        for i, k in enumerate((1, 2, -1)):
            for c in range(4):
                x_ref[4 * i + c, r] = ahead(w_ref[0, c, r], k)
            x_ref[12 + i, r] = ahead(p_ref[0, 0, r], k)
        x_ref[15, r] = ahead(p_ref[0, 2, r], 1)
        x_ref[16, r] = ahead(p_ref[0, 3, r], 1)

    return shifted


def along_rows(w_ref, p_ref, d_ref, tiles, lo, hi, unroll):
    def flux(t, r):
        w = [w_ref[t, c, r] for c in range(4)]
        press, q, sound = p_ref[t, 0, r], p_ref[t, 1, r], p_ref[t, 3, r]
        f = [w[1], w[1] * q + press, w[2] * q, (w[3] + press) * q]
        return f, jnp.abs(q) + sound

    def sensor(t, r):
        return quarter_sensor(p_ref[t, 0, r - 1], p_ref[t, 0, r], p_ref[t, 0, r + 1])

    def diff(t, r):
        return [w_ref[t, c, r + 1] - w_ref[t, c, r] for c in range(4)]

    def face(t, r, d_back, d_here, f_here, s_here, n_here):
        d_next = diff(t, r + 1)
        f_next, s_next = flux(t, r + 1)
        n_next = sensor(t, r + 1)
        ca, cb = face_coefs(n_here, n_next, s_here, s_next)
        h = [
            f_here[c] + f_next[c] - ca * d_here[c] + cb * (d_next[c] + d_back[c])
            for c in range(4)
        ]
        return h, d_next, f_next, s_next, n_next

    for t in range(tiles):
        d_back = diff(t, lo - 2)
        d_here = diff(t, lo - 1)
        f_here, s_here = flux(t, lo - 1)
        n_here = sensor(t, lo - 1)
        h, d_next, f_next, s_next, n_next = face(t, lo - 1, d_back, d_here, f_here, s_here, n_here)

        def body(r, carry, t=t):
            h_back, d_back, d_here, f_here, s_here, n_here = carry
            h, d_next, f_next, s_next, n_next = face(t, r, d_back, d_here, f_here, s_here, n_here)
            for c in range(4):
                d_ref[t, c, r] = h[c] - h_back[c]
            return h, d_here, d_next, f_next, s_next, n_next

        loop(lo, hi, unroll, body, (h, d_here, d_next, f_next, s_next, n_next))


def lane_flux(w, press, q):
    return [w[2], w[1] * q, w[2] * q + press, (w[3] + press) * q]


def along_lanes_fine(w_ref, p_ref, d_ref, x_ref, lo, hi, ahead, emit, unroll):
    def body(r):
        we, wo = ([w_ref[t, c, r] for c in range(4)] for t in range(2))
        (pe, po), (qe, qo) = ([p_ref[t, i, r] for t in range(2)] for i in (0, 2))
        se, so = jnp.abs(qe) + p_ref[0, 3, r], jnp.abs(qo) + p_ref[1, 3, r]
        pe1, po1, pom, qe1 = x_ref[4, r], x_ref[15, r], x_ref[16, r], x_ref[5, r]
        se1 = jnp.abs(qe1) + x_ref[6, r]
        we1, wo1, wom = ([x_ref[i + c, r] for c in range(4)] for i in (0, 7, 11))
        ne = quarter_sensor(pom, pe, po)
        no = quarter_sensor(pe, po, pe1)
        ne1 = quarter_sensor(po, pe1, po1)
        ae, be = face_coefs(ne, no, se, so)
        ao, bo = face_coefs(no, ne1, so, se1)
        fe, fo, fe1 = lane_flux(we, pe, qe), lane_flux(wo, po, qo), lane_flux(we1, pe1, qe1)
        out = []
        for c in range(4):
            de = wo[c] - we[c]
            do = we1[c] - wo[c]
            he = fe[c] + fo[c] - ae * de + be * (do + (we[c] - wom[c]))
            ho = fo[c] + fe1[c] - ao * do + bo * ((wo1[c] - we1[c]) + de)
            out.append([he - ahead(ho, -1) + d_ref[0, c, r], ho - he + d_ref[1, c, r]])
        for t, w in enumerate((we, wo)):
            emit(t, r, w, [out[c][t] for c in range(4)])

    staged_loop(lo, hi, unroll, shifted_fine(w_ref, p_ref, x_ref, ahead), body)


def along_lanes_coarse(w_ref, p_ref, d_ref, x_ref, lo, hi, ahead, emit, unroll):
    def body(r):
        w = [w_ref[0, c, r] for c in range(4)]
        press, q = p_ref[0, 0, r], p_ref[0, 2, r]
        spec = jnp.abs(q) + p_ref[0, 3, r]
        p1, p2, pm = (x_ref[12 + i, r] for i in range(3))
        q1 = x_ref[15, r]
        s1 = jnp.abs(q1) + x_ref[16, r]
        w1, w2, wm = ([x_ref[4 * i + c, r] for c in range(4)] for i in range(3))
        ca, cb = face_coefs(quarter_sensor(pm, press, p1), quarter_sensor(press, p1, p2), spec, s1)
        f, f1 = lane_flux(w, press, q), lane_flux(w1, p1, q1)
        out = []
        for c in range(4):
            h = f[c] + f1[c] - ca * (w1[c] - w[c]) + cb * ((w2[c] - w1[c]) + (w[c] - wm[c]))
            out.append(h - ahead(h, -1) + d_ref[0, c, r])
        emit(0, r, w, out)

    staged_loop(lo, hi, unroll, shifted_coarse(w_ref, p_ref, x_ref, ahead), body)


def with_source(w, total, both, far, winf, half_h):
    out = []
    for c in range(4):
        base = total[c] if half_h == 1.0 else half_h * total[c]
        term = (both if c in (1, 2) else far) * w[c]
        if not (isinstance(winf[c], float) and winf[c] == 0.0):
            term = term - far * winf[c]
        out.append(base + term)
    return out


def weights(kind):
    far = jnp.where(kind == 2.0, 1.0, 0.0)
    return jnp.where(kind == 1.0, 2.0, far), far


def spectral_sum(p_ref, t, r):
    return jnp.abs(p_ref[t, 1, r]) + jnp.abs(p_ref[t, 2, r]) + 2.0 * p_ref[t, 3, r]


def leg(refs, ahead, winf, rows, refresh, offset):
    w, pr, dx, sm, fr, cs, cpr, cdx, csum, kk, seg, forc, corr, share, x = refs
    (p1, s1, p2, s2, c_state, c_seg, c_prim, c_out) = rows

    def smooth(t, r, mine, total):
        both, far = weights(w[t, 4, r])
        res = with_source(mine, total, both, far, winf(), 0.5)
        scale = 0.4 / spectral_sum(pr, t, r)
        for c in range(4):
            sm[t, c, r] = mine[c] - scale * res[c]

    def fine(t, r, mine, total):
        both, far = weights(w[t, 4, r])
        res = with_source(mine, total, both, far, winf(), 0.5)
        for c in range(4):
            fr[t, c, r] = res[c]

    primitives(w, pr, 2, *p1)
    along_rows(w, pr, dx, 2, *s1, ROW_UNROLL)
    yield "rows"
    along_lanes_fine(w, pr, dx, x, *s1, ahead, smooth, FINE_UNROLL)
    refresh(sm)
    yield "smoothed"
    primitives(sm, pr, 2, *p2)
    along_rows(sm, pr, dx, 2, *s2, ROW_UNROLL)
    along_lanes_fine(sm, pr, dx, x, *s2, ahead, fine, FINE_UNROLL)
    yield "fine"

    def four(get, k):
        i = 2 * k + offset
        return (get(0, i) + get(0, i + 1)) + (get(1, i) + get(1, i + 1))

    def state(k, carry):
        for c in range(4):
            cs[0, c, k] = 0.25 * four(lambda t, i: sm[t, c, i], k)
        return carry

    loop(*c_state, 4, state)
    refresh(cs)

    def sums(k, carry):
        for c in range(4):
            csum[0, c, k] = four(lambda t, i: fr[t, c, i], k)
        for j in range(2):
            share[0, j, k] = four(lambda t, i: weights(w[t, 4, i])[j], k)
        return carry

    loop(*c_seg, 4, sums)
    primitives(cs, cpr, 1, *c_prim)

    def segment(k, carry):
        scale = 0.2 / spectral_sum(cpr, 0, k)
        kk[0, k] = scale
        for c in range(4):
            seg[0, c, k] = cs[0, c, k] - scale * csum[0, c, k]
        return carry

    loop(*c_seg, 4, segment)
    refresh(seg)

    def coarse_residual(k, mine, total):
        return with_source(mine, total, share[0, 0, k], share[0, 1, k], winf(), 1.0)

    def force(t, k, mine, total):
        res = coarse_residual(k, mine, total)
        for c in range(4):
            forc[0, c, k] = csum[0, c, k] - res[c]

    along_rows(cs, cpr, cdx, 1, *c_out, ROW_UNROLL)
    along_lanes_coarse(cs, cpr, cdx, x, *c_out, ahead, force, COARSE_UNROLL)
    primitives(seg, cpr, 1, *c_prim)

    def final(t, k, mine, total):
        res = coarse_residual(k, mine, total)
        for c in range(4):
            corr[0, c, k] = -kk[0, k] * (res[c] + forc[0, c, k])

    along_rows(seg, cpr, cdx, 1, *c_out, ROW_UNROLL)
    along_lanes_coarse(seg, cpr, cdx, x, *c_out, ahead, final, COARSE_UNROLL)
    yield "done"


MAIN_ROWS = ((0, 36), (2, 34), (0, 36), (2, 34), (2, 18), (2, 18), (0, 20), (2, 18))
STRIP_ROWS = ((0, 24), (2, 22), (2, 22), (4, 20), (2, 10), (2, 10), (2, 10), (4, 8))


def winf_main():
    return (1.0, 0.5, 0.0, ENERGY)


def winf_strip():
    column = sub_index() <= RIGHT
    return (1.0, jnp.where(column, 0.0, 0.5), jnp.where(column, 0.5, 0.0), ENERGY)


def refresh_main(ref):
    depth = ref.shape[2]
    for t in range(ref.shape[0]):
        for c in range(4):
            for i in range(2):
                ref[t, c, i] = sub_roll(ref[t, c, depth - 4 + i], 1)
                ref[t, c, depth - 2 + i] = sub_roll(ref[t, c, 2 + i], -1)


def no_refresh(ref):
    pass


def run_to(steps, name):
    for reached in steps:
        if reached == name:
            return


def kernel(nx, ny, flow_hbm, kind_hbm, out_new, out_res, raw, raw_kind, nat, nat_kind, columns, pack, got, rows_got,
           columns_got, col_in, col_turned, spread, *rest):
    main_refs, strip_refs, sems = rest[:15], rest[15:30], rest[30:]
    load_sem, send_sem, recv_sem = sems
    gx, gy = lax.axis_index("gx"), lax.axis_index("gy")
    up, down = lax.rem(gx + nx - 1, nx), lax.rem(gx + 1, nx)
    left, right = lax.rem(gy + ny - 1, ny), lax.rem(gy + 1, ny)
    neighbours = [(up, gy), (down, gy), (gx, left), (gx, right), (up, left), (up, right), (down, left), (down, right)]
    barrier = pltpu.get_barrier_semaphore()
    for where in neighbours:
        pl.semaphore_signal(barrier, inc=1, device_id=where, device_id_type=MESH)

    loads = []

    def load(src, dst):
        copy = pltpu.make_async_copy(src, dst, load_sem.at[len(loads)])
        copy.start()
        loads.append(copy)

    for t in range(2):
        cols = pl.ds(t * LANES, LANES)
        load(flow_hbm.at[:, :, cols], nat.at[t])
        load(kind_hbm.at[:, cols], nat_kind.at[t])
    natural = len(loads)
    for t in range(2):
        cols = pl.ds(t * LANES, LANES)
        for s in range(SUB):
            rows = pl.ds(ROWS * s, ROWS)
            load(flow_hbm.at[:, rows, cols], raw.at[t, :, :, s, :])
            load(kind_hbm.at[rows, cols], raw_kind.at[t, :, s, :])

    w_main, w_strip = main_refs[0], strip_refs[0]
    lane = lane_index()

    for copy in loads[:natural]:
        copy.wait()

    for side in range(2):
        for i, row in enumerate((0, 8, 240, 248)):
            rows = pl.ds(row, 8)
            total = None
            for c in range(5):
                v = nat_kind[side, rows, :].astype(jnp.float32) if c == 4 else nat[side, c, rows, :]
                v = pltpu.roll(v, 8 * (c + side), 1)
                total = v if c == 0 else jnp.where(lane >= 8 * c, v, total)
            group = lane // 8
            pack[side, pl.ds(8 * i, 8), :] = take(total, 8 * (group // 2) + 2 * (lane % 4) + group % 2)

    number = 0
    copies = []

    def send(src, dst, where):
        nonlocal number
        copy = pltpu.make_async_remote_copy(
            src_ref=src, dst_ref=dst, send_sem=send_sem.at[number], recv_sem=recv_sem.at[number],
            device_id=where, device_id_type=MESH)
        copy.start()
        copies.append(copy)
        number += 1

    for copy in loads[natural:]:
        copy.wait()

    for t in range(2):
        low = lane < LANES // 2
        index = jnp.bitwise_and(2 * lane + t, LANES - 1)

        def part(r, carry):
            for c in range(5):
                a, b = (raw_kind[s, r].astype(jnp.float32) if c == 4 else raw[s, c, r] for s in range(2))
                w_main[t, c, r + 2] = jnp.where(low, take(a, index), take(b, index))
            return carry

        loop(0, ROWS, PART_UNROLL, part)

    for c, source in enumerate((0, 2, 1, 3, 4)):
        for side in range(2):
            for t in range(2):
                rows = pl.ds(t, LANES, stride=2)
                v = nat_kind[side, rows, :].astype(jnp.float32) if c == 4 else nat[side, source, rows, :]
                turned = v.T
                columns[side, t, c] = turned[112:128] if side else turned[0:16]

    column = lax.broadcasted_iota(jnp.int32, (2 * LANES, 2 * LANES), 1)
    source = lax.broadcasted_iota(jnp.int32, (2 * LANES, 2 * LANES), 0)
    ones = jnp.where(column == 2 * (source % LANES) + source // LANES, 1.0, 0.0).astype(jnp.bfloat16)
    for i in range(3):
        spread[pl.ds(2 * LANES * i, 2 * LANES), :] = ones

    def own(base):
        def body(i, carry):
            sub = sub_index()
            r = i + base
            for t in range(2):
                for c in range(5):
                    v = jnp.zeros((SUB, LANES), jnp.float32)
                    if base >= 8:
                        v = jnp.where(sub == TOP, sub_roll(w_main[t, c, r - 6], TOP), v)
                        v = jnp.where(sub == LEFT, jnp.broadcast_to(columns[0, t, c, pl.ds(r - 8, 1), :], (SUB, LANES)), v)
                    if base <= 8:
                        v = jnp.where(sub == BOT, sub_roll(w_main[t, c, r + 18], BOT - 7), v)
                        v = jnp.where(sub == RIGHT, jnp.broadcast_to(columns[1, t, c, pl.ds(r, 1), :], (SUB, LANES)), v)
                    w_strip[t, c, r] = v
            return carry

        loop(0, 8, 4, body)

    def arrived(base):
        def body(i, carry):
            sub = sub_index()
            r = i + base
            total = jnp.zeros((SUB, LANES), jnp.float32)
            for where, side, row in ((TOP_L, 0, r), (TOP_R, 1, r), (BOT_L, 0, r + 24), (BOT_R, 1, r + 24)):
                total = jnp.where(sub == where, jnp.broadcast_to(got[side, pl.ds(row, 1), :], (SUB, LANES)), total)
            at_halo = jnp.logical_and(sub >= TOP_L, jnp.logical_and(sub != TOP, sub != BOT))
            for t in range(2):
                for c in range(5):
                    v = jnp.where(at_halo, pltpu.roll(total, -(8 * (2 * c + t) + 4) % LANES, 1), w_strip[t, c, r])
                    for k, first, at_row, at_column in ((0, 0, TOP, LEFT), (1, 16, BOT, RIGHT)):
                        if base == first:
                            v = jnp.where(sub == at_row, jnp.broadcast_to(rows_got[k, t, c, pl.ds(i, 1), :], (SUB, LANES)), v)
                            v = jnp.where(
                                sub == at_column, jnp.broadcast_to(columns_got[k, t, c, pl.ds(i, 1), :], (SUB, LANES)), v)
                    w_strip[t, c, r] = v
            return carry

        loop(0, 8, 4, body)

    refresh_main(w_main)
    main = leg(main_refs, ahead_main, winf_main, MAIN_ROWS, refresh_main, -2)
    run_to(main, "smoothed")
    pl.semaphore_wait(barrier, 8)
    send(pack.at[1, pl.ds(24, 8)], got.at[0, pl.ds(0, 8)], (down, right))
    send(pack.at[0, pl.ds(24, 8)], got.at[1, pl.ds(0, 8)], (down, left))
    send(pack.at[1, pl.ds(0, 8)], got.at[0, pl.ds(40, 8)], (up, right))
    send(pack.at[0, pl.ds(0, 8)], got.at[1, pl.ds(40, 8)], (up, left))
    send(w_main.at[:, :, pl.ds(26, 8), 7, :], rows_got.at[0], (down, gy))
    send(w_main.at[:, :, pl.ds(2, 8), 0, :], rows_got.at[1], (up, gy))
    send(pack.at[1], got.at[0, pl.ds(8, 32)], (gx, right))
    send(pack.at[0], got.at[1, pl.ds(8, 32)], (gx, left))
    send(columns.at[1, :, :, pl.ds(8, 8), :], columns_got.at[0], (gx, right))
    send(columns.at[0, :, :, pl.ds(0, 8), :], columns_got.at[1], (gx, left))
    for base in (0, 8, 16):
        own(base)
    run_to(main, "done")

    sm_main, fr_main, corr_main = main_refs[3], main_refs[4], main_refs[12]
    sm_strip, fr_strip, corr_strip = strip_refs[3], strip_refs[4], strip_refs[12]

    def in_order(even, odd):
        x = jnp.concatenate([jnp.concatenate(even, 0), jnp.concatenate(odd, 0)], 1)
        high = x.astype(jnp.bfloat16)
        rest = x - high.astype(jnp.float32)
        middle = rest.astype(jnp.bfloat16)
        low = (rest - middle.astype(jnp.float32)).astype(jnp.bfloat16)
        return jnp.dot(jnp.concatenate([high, middle, low], 1), spread[...], preferred_element_type=jnp.float32)

    def join_main(c, carry):
        for out in (out_new, out_res):
            for half in range(2):
                span = range(16 * half, 16 * half + 16)
                if out is out_new:
                    tiles = [[sm_main[t, c, r + 2] + corr_main[0, c, r // 2 + 2] for r in span] for t in range(2)]
                else:
                    tiles = [[fr_main[t, c, r + 2] for r in span] for t in range(2)]
                y = in_order(*tiles)
                for tile in range(2):
                    for i, r in enumerate(span):
                        out[tile, c, r] = y[8 * i : 8 * i + 8, LANES * tile : LANES * tile + LANES]
        return carry

    lax.fori_loop(0, 4, join_main, 0)

    for copy in copies:
        copy.wait_recv()
    for base in (0, 8, 16):
        arrived(base)
    run_to(leg(strip_refs, ahead_strip, winf_strip, STRIP_ROWS, no_refresh, 0), "done")

    for i in range(8):
        for t in range(2):
            for c, target in enumerate((0, 2, 1, 3)):
                for a, v in (
                    (target, sm_strip[t, c, i + 8] + corr_strip[0, c, (i + 8) // 2]),
                    (target + 4, fr_strip[t, c, i + 8]),
                ):
                    col_in[t, pl.ds(16 * a + 8 + i, 1), :] = v[LEFT : LEFT + 1]
                    col_in[t, pl.ds(16 * a + i, 1), :] = v[RIGHT : RIGHT + 1]
    for t in range(2):
        col_turned[t] = col_in[t].T

    def sides(k, carry):
        lane = lane_index()
        for i in range(2):
            side = col_turned[i, pl.ds(k, SUB, stride=16), :]
            r = 2 * k + i
            for a in range(8):
                out, c = (out_new, a) if a < 4 else (out_res, a - 4)
                v = pltpu.roll(side, -(16 * a + 8) % LANES, 1)
                out[0, c, r] = jnp.where(lane < 8, v, out[0, c, r])
                out[1, c, r] = jnp.where(lane >= LANES - 8, v, out[1, c, r])
        return carry

    loop(0, 16, 4, sides)

    def ends(c, carry):
        sub = sub_index()
        for out in (out_new, out_res):
            if out is out_new:
                tiles = [[sm_strip[t, c, r] + corr_strip[0, c, r // 2] for r in range(8, 16)] for t in range(2)]
            else:
                tiles = [[fr_strip[t, c, r] for r in range(8, 16)] for t in range(2)]
            y = in_order(*tiles)
            for tile in range(2):
                for r in range(8):
                    v = y[8 * r : 8 * r + 8, LANES * tile : LANES * tile + LANES]
                    out[tile, c, r] = jnp.where(sub == 0, sub_roll(v, -TOP), out[tile, c, r])
                    out[tile, c, r + 24] = jnp.where(sub == 7, sub_roll(v, 7 - BOT), out[tile, c, r + 24])
        return carry

    lax.fori_loop(0, 4, ends, 0)
    for copy in copies:
        copy.wait_send()


def put_kernel(new, res, new_hbm, res_hbm, sems):
    copies = []
    for src, dst in ((new, new_hbm), (res, res_hbm)):
        for t in range(2):
            for s in range(SUB):
                copy = pltpu.make_async_copy(
                    src.at[t, :, :, s, :], dst.at[:, pl.ds(ROWS * s, ROWS), pl.ds(t * LANES, LANES)], sems.at[len(copies)])
                copy.start()
                copies.append(copy)
    for copy in copies:
        copy.wait()


def vmem(*shape):
    return pltpu.VMEM(shape, jnp.float32)


def domain(rows, coarse_rows):
    tile = (SUB, LANES)
    return [
        vmem(2, 5, rows, *tile),
        vmem(2, 4, rows, *tile),
        vmem(2, 4, rows, *tile),
        vmem(2, 4, rows, *tile),
        vmem(2, 4, rows, *tile),
        vmem(1, 4, coarse_rows, *tile),
        vmem(1, 4, coarse_rows, *tile),
        vmem(1, 4, coarse_rows, *tile),
        vmem(1, 4, coarse_rows, *tile),
        vmem(1, coarse_rows, *tile),
        vmem(1, 4, coarse_rows, *tile),
        vmem(1, 4, coarse_rows, *tile),
        vmem(1, 4, coarse_rows, *tile),
        vmem(1, 2, coarse_rows, *tile),
        vmem(17, rows, *tile),
    ]


def solution(mesh):
    nx, ny = mesh.shape["gx"], mesh.shape["gy"]

    def local(flow_state, cell_kind):
        hbm = pl.BlockSpec(memory_space=pl.ANY)
        held = pl.BlockSpec(memory_space=pltpu.VMEM)
        block = (2, 4, ROWS, SUB, LANES)
        new, res = pl.pallas_call(
            functools.partial(kernel, nx, ny),
            out_shape=(vmem(*block), vmem(*block)),
            in_specs=[hbm, hbm],
            out_specs=(held, held),
            scratch_shapes=[
                vmem(*block),
                pltpu.VMEM((2, ROWS, SUB, LANES), jnp.int32),
                vmem(2, 4, 256, LANES),
                pltpu.VMEM((2, 256, LANES), jnp.int32),
                vmem(2, 2, 5, 16, LANES),
                vmem(2, 32, LANES),
                vmem(2, 48, LANES),
                vmem(2, 2, 5, 8, LANES),
                vmem(2, 2, 5, 8, LANES),
                vmem(2, LANES, LANES),
                vmem(2, LANES, LANES),
                pltpu.VMEM((6 * LANES, 2 * LANES), jnp.bfloat16),
                *domain(36, 20),
                *domain(24, 12),
                pltpu.SemaphoreType.DMA((36,)),
                pltpu.SemaphoreType.DMA((10,)),
                pltpu.SemaphoreType.DMA((10,)),
            ],
            compiler_params=pltpu.CompilerParams(
                collective_id=0, has_side_effects=True, vmem_limit_bytes=64_900_000
            ),
        )(flow_state, cell_kind)
        out = jax.ShapeDtypeStruct(flow_state.shape, jnp.float32)
        return pl.pallas_call(
            put_kernel,
            out_shape=(out, out),
            in_specs=[hbm, hbm],
            out_specs=(hbm, hbm),
            scratch_shapes=[pltpu.SemaphoreType.DMA((32,))],
            compiler_params=pltpu.CompilerParams(vmem_limit_bytes=1 << 20),
        )(new, res)

    return jax.shard_map(
        local,
        mesh=mesh,
        in_specs=(P(None, "gx", "gy"), P("gx", "gy")),
        out_specs=(P(None, "gx", "gy"), P(None, "gx", "gy")),
        check_vma=False,
    )
```

```python
import functools

import jax
import jax.numpy as jnp
from jax import lax
from jax.experimental import pallas as pl
from jax.experimental.pallas import tpu as pltpu
from jax.sharding import PartitionSpec as P

MESH = pl.DeviceIdType.MESH
LANES = 128
SUB = 8
ROWS = 32
STRIP = 24

ENERGY = 1.0 / 0.56 + 0.125

LEFT, RIGHT, TOP_L, TOP, TOP_R, BOT_L, BOT, BOT_R = range(8)

FINE_UNROLL = 4
JOIN_UNROLL = 8
PART_UNROLL = 16
ROW_UNROLL = 8
COARSE_UNROLL = 4


def lane_index():
    return lax.broadcasted_iota(jnp.int32, (SUB, LANES), 1)


def sub_index():
    return lax.broadcasted_iota(jnp.int32, (SUB, LANES), 0)


def sub_roll(v, shift):
    return pltpu.roll(v, shift % SUB, 0)


def take(v, index):
    return jnp.take_along_axis(v, index, axis=1)


def ahead_main(v, k):
    return pltpu.roll(v, -k % LANES, 1)


def ahead_strip(v, k):
    here = pltpu.roll(v, -k % LANES, 1)
    lane = lane_index()
    if k > 0:
        return jnp.where(lane >= LANES - k, sub_roll(here, -1), here)
    return jnp.where(lane < -k, sub_roll(here, 1), here)


def loop(lo, hi, unroll, body, carry=0):
    count = hi - lo
    while count % unroll:
        unroll -= 1

    def run(step, carry):
        for i in range(unroll):
            carry = body(lo + step * unroll + i, carry)
        return carry

    return lax.fori_loop(0, count // unroll, run, carry)


def staged_loop(lo, hi, unroll, prepare, body):
    count = hi - lo
    while count % unroll:
        unroll -= 1
    for i in range(unroll):
        prepare(lo + i)

    def run(step, carry):
        first = lo + step * unroll
        for i in range(unroll):
            prepare(first + unroll + i)
        for i in range(unroll):
            body(first + i)
        return carry

    lax.fori_loop(0, count // unroll - 1, run, 0)
    for i in range(unroll):
        body(hi - unroll + i)


def primitives(w_ref, p_ref, tiles, lo, hi, unroll=4):
    def body(r, carry):
        for t in range(tiles):
            density, mom_r, mom_l, energy = (w_ref[t, c, r] for c in range(4))
            inverse = 1.0 / density
            u = mom_r * inverse
            v = mom_l * inverse
            press = 0.4 * (energy - 0.5 * (mom_r * u + mom_l * v))
            p_ref[t, 0, r] = press
            p_ref[t, 1, r] = u
            p_ref[t, 2, r] = v
            p_ref[t, 3, r] = jnp.sqrt(1.4 * press * inverse)
        return carry

    loop(lo, hi, unroll, body)


def face_coefs(sensor_a, sensor_b, spec_a, spec_b):
    second = jnp.maximum(sensor_a, sensor_b)
    fourth = jnp.maximum(0.0, 1.0 / 32.0 - second)
    total = spec_a + spec_b
    coef_b = total * fourth
    coef_a = total * second + 2.0 * coef_b
    return coef_a, coef_b


def quarter_sensor(low, mid, high):
    ends = low + high
    twice = 2.0 * mid
    return 0.25 * jnp.abs(ends - twice) / (ends + twice)


def shifted_fine(w_ref, p_ref, x_ref, ahead):
    def shifted(r):
        for c in range(4):
            x_ref[c, r] = ahead(w_ref[0, c, r], 1)
        for i, j in enumerate((0, 2, 3)):
            x_ref[4 + i, r] = ahead(p_ref[0, j, r], 1)
        for c in range(4):
            x_ref[7 + c, r] = ahead(w_ref[1, c, r], 1)
            x_ref[11 + c, r] = ahead(w_ref[1, c, r], -1)
        x_ref[15, r] = ahead(p_ref[1, 0, r], 1)
        x_ref[16, r] = ahead(p_ref[1, 0, r], -1)

    return shifted


def shifted_coarse(w_ref, p_ref, x_ref, ahead):
    def shifted(r):
        for i, k in enumerate((1, 2, -1)):
            for c in range(4):
                x_ref[4 * i + c, r] = ahead(w_ref[0, c, r], k)
            x_ref[12 + i, r] = ahead(p_ref[0, 0, r], k)
        x_ref[15, r] = ahead(p_ref[0, 2, r], 1)
        x_ref[16, r] = ahead(p_ref[0, 3, r], 1)

    return shifted


def along_rows(w_ref, p_ref, d_ref, tiles, lo, hi, unroll):
    def flux(t, r):
        w = [w_ref[t, c, r] for c in range(4)]
        press, q, sound = p_ref[t, 0, r], p_ref[t, 1, r], p_ref[t, 3, r]
        f = [w[1], w[1] * q + press, w[2] * q, (w[3] + press) * q]
        return f, jnp.abs(q) + sound

    def sensor(t, r):
        return quarter_sensor(p_ref[t, 0, r - 1], p_ref[t, 0, r], p_ref[t, 0, r + 1])

    def diff(t, r):
        return [w_ref[t, c, r + 1] - w_ref[t, c, r] for c in range(4)]

    def face(t, r, d_back, d_here, f_here, s_here, n_here):
        d_next = diff(t, r + 1)
        f_next, s_next = flux(t, r + 1)
        n_next = sensor(t, r + 1)
        ca, cb = face_coefs(n_here, n_next, s_here, s_next)
        h = [
            f_here[c] + f_next[c] - ca * d_here[c] + cb * (d_next[c] + d_back[c])
            for c in range(4)
        ]
        return h, d_next, f_next, s_next, n_next

    for t in range(tiles):
        d_back = diff(t, lo - 2)
        d_here = diff(t, lo - 1)
        f_here, s_here = flux(t, lo - 1)
        n_here = sensor(t, lo - 1)
        h, d_next, f_next, s_next, n_next = face(t, lo - 1, d_back, d_here, f_here, s_here, n_here)

        def body(r, carry, t=t):
            h_back, d_back, d_here, f_here, s_here, n_here = carry
            h, d_next, f_next, s_next, n_next = face(t, r, d_back, d_here, f_here, s_here, n_here)
            for c in range(4):
                d_ref[t, c, r] = h[c] - h_back[c]
            return h, d_here, d_next, f_next, s_next, n_next

        loop(lo, hi, unroll, body, (h, d_here, d_next, f_next, s_next, n_next))


def lane_flux(w, press, q):
    return [w[2], w[1] * q, w[2] * q + press, (w[3] + press) * q]


def along_lanes_fine(w_ref, p_ref, d_ref, x_ref, lo, hi, ahead, emit, unroll):
    def body(r):
        we, wo = ([w_ref[t, c, r] for c in range(4)] for t in range(2))
        (pe, po), (qe, qo) = ([p_ref[t, i, r] for t in range(2)] for i in (0, 2))
        se, so = jnp.abs(qe) + p_ref[0, 3, r], jnp.abs(qo) + p_ref[1, 3, r]
        pe1, po1, pom, qe1 = x_ref[4, r], x_ref[15, r], x_ref[16, r], x_ref[5, r]
        se1 = jnp.abs(qe1) + x_ref[6, r]
        we1, wo1, wom = ([x_ref[i + c, r] for c in range(4)] for i in (0, 7, 11))
        ne = quarter_sensor(pom, pe, po)
        no = quarter_sensor(pe, po, pe1)
        ne1 = quarter_sensor(po, pe1, po1)
        ae, be = face_coefs(ne, no, se, so)
        ao, bo = face_coefs(no, ne1, so, se1)
        fe, fo, fe1 = lane_flux(we, pe, qe), lane_flux(wo, po, qo), lane_flux(we1, pe1, qe1)
        out = []
        for c in range(4):
            de = wo[c] - we[c]
            do = we1[c] - wo[c]
            he = fe[c] + fo[c] - ae * de + be * (do + (we[c] - wom[c]))
            ho = fo[c] + fe1[c] - ao * do + bo * ((wo1[c] - we1[c]) + de)
            out.append([he - ahead(ho, -1) + d_ref[0, c, r], ho - he + d_ref[1, c, r]])
        for t, w in enumerate((we, wo)):
            emit(t, r, w, [out[c][t] for c in range(4)])

    staged_loop(lo, hi, unroll, shifted_fine(w_ref, p_ref, x_ref, ahead), body)


def along_lanes_coarse(w_ref, p_ref, d_ref, x_ref, lo, hi, ahead, emit, unroll):
    def body(r):
        w = [w_ref[0, c, r] for c in range(4)]
        press, q = p_ref[0, 0, r], p_ref[0, 2, r]
        spec = jnp.abs(q) + p_ref[0, 3, r]
        p1, p2, pm = (x_ref[12 + i, r] for i in range(3))
        q1 = x_ref[15, r]
        s1 = jnp.abs(q1) + x_ref[16, r]
        w1, w2, wm = ([x_ref[4 * i + c, r] for c in range(4)] for i in range(3))
        ca, cb = face_coefs(quarter_sensor(pm, press, p1), quarter_sensor(press, p1, p2), spec, s1)
        f, f1 = lane_flux(w, press, q), lane_flux(w1, p1, q1)
        out = []
        for c in range(4):
            h = f[c] + f1[c] - ca * (w1[c] - w[c]) + cb * ((w2[c] - w1[c]) + (w[c] - wm[c]))
            out.append(h - ahead(h, -1) + d_ref[0, c, r])
        emit(0, r, w, out)

    staged_loop(lo, hi, unroll, shifted_coarse(w_ref, p_ref, x_ref, ahead), body)


def with_source(w, total, both, far, winf, half_h):
    out = []
    for c in range(4):
        base = total[c] if half_h == 1.0 else half_h * total[c]
        term = (both if c in (1, 2) else far) * w[c]
        if not (isinstance(winf[c], float) and winf[c] == 0.0):
            term = term - far * winf[c]
        out.append(base + term)
    return out


def weights(kind):
    far = jnp.where(kind == 2.0, 1.0, 0.0)
    return jnp.where(kind == 1.0, 2.0, far), far


def spectral_sum(p_ref, t, r):
    return jnp.abs(p_ref[t, 1, r]) + jnp.abs(p_ref[t, 2, r]) + 2.0 * p_ref[t, 3, r]


def leg(refs, ahead, winf, rows, refresh, offset):
    w, pr, dx, sm, fr, cs, cpr, cdx, csum, kk, seg, forc, corr, share, x = refs
    (p1, s1, p2, s2, c_state, c_seg, c_prim, c_out) = rows

    def smooth(t, r, mine, total):
        both, far = weights(w[t, 4, r])
        res = with_source(mine, total, both, far, winf(), 0.5)
        scale = 0.4 / spectral_sum(pr, t, r)
        for c in range(4):
            sm[t, c, r] = mine[c] - scale * res[c]

    def fine(t, r, mine, total):
        both, far = weights(w[t, 4, r])
        res = with_source(mine, total, both, far, winf(), 0.5)
        for c in range(4):
            fr[t, c, r] = res[c]

    primitives(w, pr, 2, *p1)
    along_rows(w, pr, dx, 2, *s1, ROW_UNROLL)
    yield "rows"
    along_lanes_fine(w, pr, dx, x, *s1, ahead, smooth, FINE_UNROLL)
    refresh(sm)
    yield "smoothed"
    primitives(sm, pr, 2, *p2)
    along_rows(sm, pr, dx, 2, *s2, ROW_UNROLL)
    along_lanes_fine(sm, pr, dx, x, *s2, ahead, fine, FINE_UNROLL)
    yield "fine"

    def four(get, k):
        i = 2 * k + offset
        return (get(0, i) + get(0, i + 1)) + (get(1, i) + get(1, i + 1))

    def state(k, carry):
        for c in range(4):
            cs[0, c, k] = 0.25 * four(lambda t, i: sm[t, c, i], k)
        return carry

    loop(*c_state, 4, state)
    refresh(cs)

    def sums(k, carry):
        for c in range(4):
            csum[0, c, k] = four(lambda t, i: fr[t, c, i], k)
        for j in range(2):
            share[0, j, k] = four(lambda t, i: weights(w[t, 4, i])[j], k)
        return carry

    loop(*c_seg, 4, sums)
    primitives(cs, cpr, 1, *c_prim)

    def segment(k, carry):
        scale = 0.2 / spectral_sum(cpr, 0, k)
        kk[0, k] = scale
        for c in range(4):
            seg[0, c, k] = cs[0, c, k] - scale * csum[0, c, k]
        return carry

    loop(*c_seg, 4, segment)
    refresh(seg)

    def coarse_residual(k, mine, total):
        return with_source(mine, total, share[0, 0, k], share[0, 1, k], winf(), 1.0)

    def force(t, k, mine, total):
        res = coarse_residual(k, mine, total)
        for c in range(4):
            forc[0, c, k] = csum[0, c, k] - res[c]

    along_rows(cs, cpr, cdx, 1, *c_out, ROW_UNROLL)
    along_lanes_coarse(cs, cpr, cdx, x, *c_out, ahead, force, COARSE_UNROLL)
    primitives(seg, cpr, 1, *c_prim)

    def final(t, k, mine, total):
        res = coarse_residual(k, mine, total)
        for c in range(4):
            corr[0, c, k] = -kk[0, k] * (res[c] + forc[0, c, k])

    along_rows(seg, cpr, cdx, 1, *c_out, ROW_UNROLL)
    along_lanes_coarse(seg, cpr, cdx, x, *c_out, ahead, final, COARSE_UNROLL)
    yield "done"


MAIN_ROWS = ((0, 36), (2, 34), (0, 36), (2, 34), (2, 18), (2, 18), (0, 20), (2, 18))
STRIP_ROWS = ((0, 24), (2, 22), (2, 22), (4, 20), (2, 10), (2, 10), (2, 10), (4, 8))


def winf_main():
    return (1.0, 0.5, 0.0, ENERGY)


def winf_strip():
    column = sub_index() <= RIGHT
    return (1.0, jnp.where(column, 0.0, 0.5), jnp.where(column, 0.5, 0.0), ENERGY)


def refresh_main(ref):
    depth = ref.shape[2]
    for t in range(ref.shape[0]):
        for c in range(4):
            for i in range(2):
                ref[t, c, i] = sub_roll(ref[t, c, depth - 4 + i], 1)
                ref[t, c, depth - 2 + i] = sub_roll(ref[t, c, 2 + i], -1)


def no_refresh(ref):
    pass


def run_to(steps, name):
    for reached in steps:
        if reached == name:
            return


def kernel(nx, ny, flow_hbm, kind_hbm, out_new, out_res, raw, raw_kind, nat, nat_kind, columns, pack, got, rows_got,
           columns_got, col_in, col_turned, spread, *rest):
    main_refs, strip_refs, sems = rest[:15], rest[15:30], rest[30:]
    load_sem, send_sem, recv_sem = sems
    gx, gy = lax.axis_index("gx"), lax.axis_index("gy")
    up, down = lax.rem(gx + nx - 1, nx), lax.rem(gx + 1, nx)
    left, right = lax.rem(gy + ny - 1, ny), lax.rem(gy + 1, ny)
    neighbours = [(up, gy), (down, gy), (gx, left), (gx, right), (up, left), (up, right), (down, left), (down, right)]
    barrier = pltpu.get_barrier_semaphore()
    for where in neighbours:
        pl.semaphore_signal(barrier, inc=1, device_id=where, device_id_type=MESH)

    loads = []

    def load(src, dst):
        copy = pltpu.make_async_copy(src, dst, load_sem.at[len(loads)])
        copy.start()
        loads.append(copy)

    for t in range(2):
        cols = pl.ds(t * LANES, LANES)
        load(flow_hbm.at[:, :, cols], nat.at[t])
        load(kind_hbm.at[:, cols], nat_kind.at[t])
    natural = len(loads)
    for t in range(2):
        cols = pl.ds(t * LANES, LANES)
        for s in range(SUB):
            rows = pl.ds(ROWS * s, ROWS)
            load(flow_hbm.at[:, rows, cols], raw.at[t, :, :, s, :])
            load(kind_hbm.at[rows, cols], raw_kind.at[t, :, s, :])

    w_main, w_strip = main_refs[0], strip_refs[0]
    lane = lane_index()

    for copy in loads[:natural]:
        copy.wait()

    for side in range(2):
        for i, row in enumerate((0, 8, 240, 248)):
            rows = pl.ds(row, 8)
            total = None
            for c in range(5):
                v = nat_kind[side, rows, :].astype(jnp.float32) if c == 4 else nat[side, c, rows, :]
                v = pltpu.roll(v, 8 * (c + side), 1)
                total = v if c == 0 else jnp.where(lane >= 8 * c, v, total)
            group = lane // 8
            pack[side, pl.ds(8 * i, 8), :] = take(total, 8 * (group // 2) + 2 * (lane % 4) + group % 2)

    number = 0
    copies = []

    def send(src, dst, where):
        nonlocal number
        copy = pltpu.make_async_remote_copy(
            src_ref=src, dst_ref=dst, send_sem=send_sem.at[number], recv_sem=recv_sem.at[number],
            device_id=where, device_id_type=MESH)
        copy.start()
        copies.append(copy)
        number += 1

    for copy in loads[natural:]:
        copy.wait()

    for t in range(2):
        low = lane < LANES // 2
        index = jnp.bitwise_and(2 * lane + t, LANES - 1)

        def part(r, carry):
            for c in range(5):
                a, b = (raw_kind[s, r].astype(jnp.float32) if c == 4 else raw[s, c, r] for s in range(2))
                w_main[t, c, r + 2] = jnp.where(low, take(a, index), take(b, index))
            return carry

        loop(0, ROWS, PART_UNROLL, part)

    for c, source in enumerate((0, 2, 1, 3, 4)):
        for side in range(2):
            for t in range(2):
                rows = pl.ds(t, LANES, stride=2)
                v = nat_kind[side, rows, :].astype(jnp.float32) if c == 4 else nat[side, source, rows, :]
                turned = v.T
                columns[side, t, c] = turned[112:128] if side else turned[0:16]

    column = lax.broadcasted_iota(jnp.int32, (2 * LANES, 2 * LANES), 1)
    source = lax.broadcasted_iota(jnp.int32, (2 * LANES, 2 * LANES), 0)
    ones = jnp.where(column == 2 * (source % LANES) + source // LANES, 1.0, 0.0).astype(jnp.bfloat16)
    for i in range(3):
        spread[pl.ds(2 * LANES * i, 2 * LANES), :] = ones

    def own(base):
        def body(i, carry):
            sub = sub_index()
            r = i + base
            for t in range(2):
                for c in range(5):
                    v = jnp.zeros((SUB, LANES), jnp.float32)
                    if base >= 8:
                        v = jnp.where(sub == TOP, sub_roll(w_main[t, c, r - 6], TOP), v)
                        v = jnp.where(sub == LEFT, jnp.broadcast_to(columns[0, t, c, pl.ds(r - 8, 1), :], (SUB, LANES)), v)
                    if base <= 8:
                        v = jnp.where(sub == BOT, sub_roll(w_main[t, c, r + 18], BOT - 7), v)
                        v = jnp.where(sub == RIGHT, jnp.broadcast_to(columns[1, t, c, pl.ds(r, 1), :], (SUB, LANES)), v)
                    w_strip[t, c, r] = v
            return carry

        loop(0, 8, 4, body)

    def arrived(base):
        def body(i, carry):
            sub = sub_index()
            r = i + base
            total = jnp.zeros((SUB, LANES), jnp.float32)
            for where, side, row in ((TOP_L, 0, r), (TOP_R, 1, r), (BOT_L, 0, r + 24), (BOT_R, 1, r + 24)):
                total = jnp.where(sub == where, jnp.broadcast_to(got[side, pl.ds(row, 1), :], (SUB, LANES)), total)
            at_halo = jnp.logical_and(sub >= TOP_L, jnp.logical_and(sub != TOP, sub != BOT))
            for t in range(2):
                for c in range(5):
                    v = jnp.where(at_halo, pltpu.roll(total, -(8 * (2 * c + t) + 4) % LANES, 1), w_strip[t, c, r])
                    for k, first, at_row, at_column in ((0, 0, TOP, LEFT), (1, 16, BOT, RIGHT)):
                        if base == first:
                            v = jnp.where(sub == at_row, jnp.broadcast_to(rows_got[k, t, c, pl.ds(i, 1), :], (SUB, LANES)), v)
                            v = jnp.where(
                                sub == at_column, jnp.broadcast_to(columns_got[k, t, c, pl.ds(i, 1), :], (SUB, LANES)), v)
                    w_strip[t, c, r] = v
            return carry

        loop(0, 8, 8, body)

    refresh_main(w_main)
    main = leg(main_refs, ahead_main, winf_main, MAIN_ROWS, refresh_main, -2)
    run_to(main, "smoothed")
    pl.semaphore_wait(barrier, 8)
    send(pack.at[1, pl.ds(24, 8)], got.at[0, pl.ds(0, 8)], (down, right))
    send(pack.at[0, pl.ds(24, 8)], got.at[1, pl.ds(0, 8)], (down, left))
    send(pack.at[1, pl.ds(0, 8)], got.at[0, pl.ds(40, 8)], (up, right))
    send(pack.at[0, pl.ds(0, 8)], got.at[1, pl.ds(40, 8)], (up, left))
    send(w_main.at[:, :, pl.ds(26, 8), 7, :], rows_got.at[0], (down, gy))
    send(w_main.at[:, :, pl.ds(2, 8), 0, :], rows_got.at[1], (up, gy))
    send(pack.at[1], got.at[0, pl.ds(8, 32)], (gx, right))
    send(pack.at[0], got.at[1, pl.ds(8, 32)], (gx, left))
    send(columns.at[1, :, :, pl.ds(8, 8), :], columns_got.at[0], (gx, right))
    send(columns.at[0, :, :, pl.ds(0, 8), :], columns_got.at[1], (gx, left))
    for base in (0, 8, 16):
        own(base)
    run_to(main, "done")

    sm_main, fr_main, corr_main = main_refs[3], main_refs[4], main_refs[12]
    sm_strip, fr_strip, corr_strip = strip_refs[3], strip_refs[4], strip_refs[12]

    def in_order(even, odd):
        x = jnp.concatenate([jnp.concatenate(even, 0), jnp.concatenate(odd, 0)], 1)
        high = x.astype(jnp.bfloat16)
        rest = x - high.astype(jnp.float32)
        middle = rest.astype(jnp.bfloat16)
        low = (rest - middle.astype(jnp.float32)).astype(jnp.bfloat16)
        return jnp.dot(jnp.concatenate([high, middle, low], 1), spread[...], preferred_element_type=jnp.float32)

    def join_main(c, carry):
        for out in (out_new, out_res):
            for half in range(2):
                span = range(16 * half, 16 * half + 16)
                if out is out_new:
                    tiles = [[sm_main[t, c, r + 2] + corr_main[0, c, r // 2 + 2] for r in span] for t in range(2)]
                else:
                    tiles = [[fr_main[t, c, r + 2] for r in span] for t in range(2)]
                y = in_order(*tiles)
                for tile in range(2):
                    for i, r in enumerate(span):
                        out[tile, c, r] = y[8 * i : 8 * i + 8, LANES * tile : LANES * tile + LANES]
        return carry

    for c in range(4):
        join_main(c, 0)

    for copy in copies:
        copy.wait_recv()
    for base in (0, 8, 16):
        arrived(base)
    run_to(leg(strip_refs, ahead_strip, winf_strip, STRIP_ROWS, no_refresh, 0), "done")

    for i in range(8):
        for t in range(2):
            for c, target in enumerate((0, 2, 1, 3)):
                for a, v in (
                    (target, sm_strip[t, c, i + 8] + corr_strip[0, c, (i + 8) // 2]),
                    (target + 4, fr_strip[t, c, i + 8]),
                ):
                    col_in[t, pl.ds(16 * a + 8 + i, 1), :] = v[LEFT : LEFT + 1]
                    col_in[t, pl.ds(16 * a + i, 1), :] = v[RIGHT : RIGHT + 1]
    for t in range(2):
        col_turned[t] = col_in[t].T

    def sides(k, carry):
        lane = lane_index()
        for i in range(2):
            side = col_turned[i, pl.ds(k, SUB, stride=16), :]
            r = 2 * k + i
            for a in range(8):
                out, c = (out_new, a) if a < 4 else (out_res, a - 4)
                v = pltpu.roll(side, -(16 * a + 8) % LANES, 1)
                out[0, c, r] = jnp.where(lane < 8, v, out[0, c, r])
                out[1, c, r] = jnp.where(lane >= LANES - 8, v, out[1, c, r])
        return carry

    loop(0, 16, 4, sides)

    def ends(c, carry):
        sub = sub_index()
        for out in (out_new, out_res):
            if out is out_new:
                tiles = [[sm_strip[t, c, r] + corr_strip[0, c, r // 2] for r in range(8, 16)] for t in range(2)]
            else:
                tiles = [[fr_strip[t, c, r] for r in range(8, 16)] for t in range(2)]
            y = in_order(*tiles)
            for tile in range(2):
                for r in range(8):
                    v = y[8 * r : 8 * r + 8, LANES * tile : LANES * tile + LANES]
                    out[tile, c, r] = jnp.where(sub == 0, sub_roll(v, -TOP), out[tile, c, r])
                    out[tile, c, r + 24] = jnp.where(sub == 7, sub_roll(v, 7 - BOT), out[tile, c, r + 24])
        return carry

    for c in range(4):
        ends(c, 0)
    for copy in copies:
        copy.wait_send()


def put_kernel(new, res, new_hbm, res_hbm, sems):
    copies = []
    for src, dst in ((new, new_hbm), (res, res_hbm)):
        for t in range(2):
            for s in range(SUB):
                copy = pltpu.make_async_copy(
                    src.at[t, :, :, s, :], dst.at[:, pl.ds(ROWS * s, ROWS), pl.ds(t * LANES, LANES)], sems.at[len(copies)])
                copy.start()
                copies.append(copy)
    for copy in copies:
        copy.wait()


def vmem(*shape):
    return pltpu.VMEM(shape, jnp.float32)


def domain(rows, coarse_rows):
    tile = (SUB, LANES)
    return [
        vmem(2, 5, rows, *tile),
        vmem(2, 4, rows, *tile),
        vmem(2, 4, rows, *tile),
        vmem(2, 4, rows, *tile),
        vmem(2, 4, rows, *tile),
        vmem(1, 4, coarse_rows, *tile),
        vmem(1, 4, coarse_rows, *tile),
        vmem(1, 4, coarse_rows, *tile),
        vmem(1, 4, coarse_rows, *tile),
        vmem(1, coarse_rows, *tile),
        vmem(1, 4, coarse_rows, *tile),
        vmem(1, 4, coarse_rows, *tile),
        vmem(1, 4, coarse_rows, *tile),
        vmem(1, 2, coarse_rows, *tile),
        vmem(17, rows, *tile),
    ]


def solution(mesh):
    nx, ny = mesh.shape["gx"], mesh.shape["gy"]

    def local(flow_state, cell_kind):
        hbm = pl.BlockSpec(memory_space=pl.ANY)
        held = pl.BlockSpec(memory_space=pltpu.VMEM)
        block = (2, 4, ROWS, SUB, LANES)
        new, res = pl.pallas_call(
            functools.partial(kernel, nx, ny),
            out_shape=(vmem(*block), vmem(*block)),
            in_specs=[hbm, hbm],
            out_specs=(held, held),
            scratch_shapes=[
                vmem(*block),
                pltpu.VMEM((2, ROWS, SUB, LANES), jnp.int32),
                vmem(2, 4, 256, LANES),
                pltpu.VMEM((2, 256, LANES), jnp.int32),
                vmem(2, 2, 5, 16, LANES),
                vmem(2, 32, LANES),
                vmem(2, 48, LANES),
                vmem(2, 2, 5, 8, LANES),
                vmem(2, 2, 5, 8, LANES),
                vmem(2, LANES, LANES),
                vmem(2, LANES, LANES),
                pltpu.VMEM((6 * LANES, 2 * LANES), jnp.bfloat16),
                *domain(36, 20),
                *domain(24, 12),
                pltpu.SemaphoreType.DMA((36,)),
                pltpu.SemaphoreType.DMA((10,)),
                pltpu.SemaphoreType.DMA((10,)),
            ],
            compiler_params=pltpu.CompilerParams(
                collective_id=0, has_side_effects=True, vmem_limit_bytes=64_900_000
            ),
        )(flow_state, cell_kind)
        out = jax.ShapeDtypeStruct(flow_state.shape, jnp.float32)
        return pl.pallas_call(
            put_kernel,
            out_shape=(out, out),
            in_specs=[hbm, hbm],
            out_specs=(hbm, hbm),
            scratch_shapes=[pltpu.SemaphoreType.DMA((32,))],
            compiler_params=pltpu.CompilerParams(vmem_limit_bytes=1 << 20),
        )(new, res)

    return jax.shard_map(
        local,
        mesh=mesh,
        in_specs=(P(None, "gx", "gy"), P("gx", "gy")),
        out_specs=(P(None, "gx", "gy"), P(None, "gx", "gy")),
        check_vma=False,
    )
```
